32 devices in a mesh: tile: 8 (over z, x), freq: 4 (over y, core).
Axes of the slice: x: 2, y: 2, z: 4, core: 2. Of those that a mesh axis runs over, the one named last changes fastest.
Arguments:
- u_tiles: bfloat16 [4, 8, 8, 40, 1024], P('freq', 'tile'), may hold values from -0.3125 to 0.3125
- v_tiles: bfloat16 [4, 8, 8, 40, 1024], P('freq', None, 'tile'), may hold values from -0.1875 to 0.1875
- tile_ranks: int32 [4, 8, 8], P('freq'), may hold values from 4 to 40, as said below
- recorded: float32 [4, 8192, 128], P('freq', 'tile')
Outputs:
- model: float32 [4, 8192, 128], P('freq', 'tile')
- residual: float32 [4, 8192, 128], P('freq', 'tile')
- gradient: float32 [4, 8192, 128], P('freq', 'tile')
The draws below stay inside these ranges and needn't reach their ends.
Inputs may be any that keep to these rules, and one draw needn't show every extreme that they name: `tile_ranks`: every draw holds a tile of rank 40 and a tile of rank 4.
All inputs are finite; a program needn't handle non-finite values.
Results may differ from the reference program's by a relative error of at most 0.02.
Values may be sent and summed in bfloat16 or wider, within the bound.
No kernel may reach another device: no remote copies, remote signals or barrier semaphores. Data moves between devices by JAX's collectives and lax.ppermute only.
A program may use at most 128 MiB of HBM per device.

```python
import math
import jax
import jax.numpy as jnp
from jax import lax

TILE_W = 1024
RANK_PAD = 40
TRACES = 128
ITERS = 2
TILES = 8
FREQS = 4


def draw_tile_ranks(key, part):
    first, second, third = jax.random.split(jax.random.fold_in(key, 11), 3)
    shape = (FREQS, TILES, TILES)
    left = jax.random.randint(first, shape, 0, RANK_PAD - 3)
    right = jax.random.randint(second, shape, 0, RANK_PAD - 3)
    divisor = max((RANK_PAD - 4) * 18 // 25, 1)
    ranks_all = jnp.minimum(4 + left * right // divisor, RANK_PAD)
    flat = ranks_all.reshape(-1)
    total = FREQS * TILES * TILES
    spot = jax.random.randint(third, (), 0, total)
    flat = flat.at[spot].set(RANK_PAD)
    flat = flat.at[(spot + 1) % total].set(4)
    return flat.reshape(shape).astype(jnp.int32)


def draw_recorded(key, part):
    first, second = jax.random.split(jax.random.fold_in(key, 23), 2)
    shape = (FREQS, TILES * TILE_W, TRACES)
    tile_of_row = (jnp.arange(TILES * TILE_W) // TILE_W).astype(jnp.float32)
    block_scale = 1.0 + 2.0 * tile_of_row / max(TILES - 1, 1)
    row_scale = jnp.exp(jax.random.uniform(second, (FREQS, TILES * TILE_W, 1), jnp.float32, 0.0, math.log(10.0)))
    base = jax.random.normal(first, shape, jnp.float32)
    return (block_scale[None, :, None] * row_scale * base).astype(jnp.float32)


def steps_of(stream_key, dims, shards, smallest, high):
    def one(axis_at, shards_of):
        heights = jax.random.uniform(jax.random.fold_in(jax.random.fold_in(stream_key, 6), axis_at), (shards_of,), jnp.float32, smallest / len(shards), high / len(shards))
        return jnp.repeat(jnp.exp(heights), dims[axis_at] // shards_of).reshape((-1,) + (1,) * (len(dims) - axis_at - 1))

    loudness = one(*shards[0])
    for cut in shards[1:]:
        loudness = loudness * one(*cut)
    return loudness


def centred(own_key, shape, spread, limit, cuts=(), held_as=jnp.bfloat16):
    drawn = spread * jax.random.normal(own_key, shape, jnp.float32)
    if cuts:
        drawn = drawn * steps_of(own_key, shape, cuts, -0.22, 0.18)
    return jnp.clip(drawn, -limit, limit).astype(held_as)


def setup_inputs(seed: int = 0) -> dict:
    seeds = jax.random.split(jax.random.key(seed), 5)
    return {
        "u_tiles": centred(seeds[0], (FREQS, TILES, TILES, RANK_PAD, TILE_W), (TILES * RANK_PAD) ** -0.5, 0.3125, ((0, 4), (1, 8))),
        "v_tiles": centred(seeds[1], (FREQS, TILES, TILES, RANK_PAD, TILE_W), TILE_W ** -0.5, 0.1875, ((0, 4), (2, 8))),
        "tile_ranks": draw_tile_ranks(jax.random.fold_in(seeds[4], 71), 0),
        "recorded": draw_recorded(jax.random.fold_in(seeds[4], 71), 0),
    }


def rank_levels(tile_ranks):
    levels = jnp.arange(RANK_PAD, dtype=jnp.int32)
    return (levels < tile_ranks[..., None]).astype(jnp.float32)


def to_wire(value):
    return lax.optimization_barrier(value.astype(jnp.bfloat16)).astype(jnp.float32)


def forward_one(u_freq, v_freq, mask_freq, direction):
    rounded = to_wire(direction).reshape(TILES, TILE_W, TRACES)

    def tile_row(pieces):
        u_row, v_row, mask_row = pieces
        coeffs = jnp.einsum("jrb,jbs->jrs", v_row.astype(jnp.float32), rounded) * mask_row[:, :, None]
        coeffs = to_wire(coeffs)
        return jnp.einsum("jrb,jrs->bs", u_row.astype(jnp.float32), coeffs)

    return lax.map(tile_row, (u_freq, v_freq, mask_freq)).reshape(TILES * TILE_W, TRACES)


def adjoint_one(u_freq, v_freq, mask_freq, resid):
    rounded = to_wire(resid).reshape(TILES, TILE_W, TRACES)

    def tile_row(total, pieces):
        u_row, v_row, mask_row, r_row = pieces
        coeffs = jnp.einsum("jrb,bs->jrs", u_row.astype(jnp.float32), r_row) * mask_row[:, :, None]
        coeffs = to_wire(coeffs)
        return total + jnp.einsum("jrb,jrs->jbs", v_row.astype(jnp.float32), coeffs), None

    start = jnp.zeros((TILES, TILE_W, TRACES), jnp.float32)
    total, unused = lax.scan(tile_row, start, (u_freq, v_freq, mask_freq, rounded))
    return total.reshape(TILES * TILE_W, TRACES)


def reference(u_tiles, v_tiles, tile_ranks, recorded):
    masks = rank_levels(tile_ranks)

    def forward(field):
        return jnp.stack([forward_one(u_tiles[f], v_tiles[f], masks[f], field[f]) for f in range(FREQS)])

    def adjoint(field):
        return jnp.stack([adjoint_one(u_tiles[f], v_tiles[f], masks[f], field[f]) for f in range(FREQS)])

    model = jnp.zeros_like(recorded)
    resid = recorded
    gradient = adjoint(resid)
    direction = gradient
    gamma = jnp.sum(gradient * gradient)
    for iteration in range(ITERS):
        image = forward(direction)
        delta = jnp.sum(image * image)
        alpha = gamma / delta
        model = model + alpha * direction
        resid = resid - alpha * image
        gradient = adjoint(resid)
        gamma_new = jnp.sum(gradient * gradient)
        direction = gradient + (gamma_new / gamma) * direction
        gamma = gamma_new
    return model, resid, gradient
```

```python
import jax
import jax.numpy as jnp
from jax import lax
from jax.sharding import PartitionSpec as P

HIGH = lax.Precision.HIGHEST


def local(u_tiles, v_tiles, tile_ranks, recorded):
    _, tile_dev, tiles, rank_pad, width = u_tiles.shape
    traces = recorded.shape[2]
    freqs = lax.axis_size("freq")
    position = lax.axis_index("tile")
    levels = jnp.arange(rank_pad, dtype=jnp.int32)
    rank_rows = lax.dynamic_slice_in_dim(tile_ranks[0], position * tile_dev, tile_dev, 0)
    rank_cols = lax.dynamic_slice_in_dim(tile_ranks[0], position * tile_dev, tile_dev, 1)
    mask_rows = (levels < rank_rows[..., None]).astype(jnp.float32)
    mask_cols = (levels < rank_cols.T[..., None]).astype(jnp.float32)
    u = u_tiles[0].reshape(tile_dev, tiles * rank_pad, width)
    v = jnp.swapaxes(v_tiles[0], 0, 1).reshape(tile_dev, tiles * rank_pad, width)
    mask_u = mask_rows.reshape(tile_dev, tiles * rank_pad, 1)
    mask_v = mask_cols.reshape(tile_dev, tiles * rank_pad, 1)

    def gram(x):
        return jnp.einsum("drb,dsb->drs", x, x, preferred_element_type=jnp.float32)

    def swap(c):
        c = c.reshape(tile_dev, tiles, rank_pad, traces)
        c = lax.all_to_all(c, "tile", split_axis=1, concat_axis=0, tiled=True)
        return jnp.swapaxes(c, 0, 1).reshape(tile_dev, tiles * rank_pad, traces)

    def apply(g, c, mask):
        return mask * jnp.einsum("drs,dst->drt", g, c, precision=HIGH)

    def dot(x, y):
        return jnp.sum(x * y, axis=(0, 1))

    field = recorded.reshape(tile_dev, width, traces)
    gram_u, gram_v = gram(u), gram(v)
    a0 = swap(mask_u * jnp.einsum("drb,dbt->drt", u, field.astype(jnp.bfloat16), preferred_element_type=jnp.float32))
    b0v = apply(gram_v, a0, mask_v)
    b0 = swap(b0v)
    a1u = apply(gram_u, b0, mask_u)
    a1 = swap(a1u)
    b1v = apply(gram_v, a1, mask_v)
    b1 = swap(b1v)
    a2u = apply(gram_u, b1, mask_u)
    parts = jnp.stack([dot(a0, b0v), dot(b0, a1u), dot(a1, b0v), dot(a1, b1v), dot(b1, a1u), dot(b1, a2u)])
    parts = jnp.pad(parts, ((0, 2), (0, 0)))
    c = a2u.reshape(tile_dev, tiles, rank_pad, traces)
    devices = tiles // tile_dev
    extra = jnp.broadcast_to(parts, (devices, 8, traces))
    packed = jnp.concatenate(
        [jnp.moveaxis(c, 0, 1).reshape(devices, tile_dev * tile_dev * rank_pad, traces), extra], axis=1
    )
    packed = lax.all_to_all(packed, "tile", split_axis=0, concat_axis=0, tiled=True)
    sums = jnp.sum(packed[:, tile_dev * tile_dev * rank_pad :], axis=0)
    a2 = packed[:, : tile_dev * tile_dev * rank_pad].reshape(devices, tile_dev, tile_dev, rank_pad, traces)
    a2 = jnp.moveaxis(a2, 1, 0).reshape(tile_dev, tiles * rank_pad, traces)
    whole = sums
    for step in range(1, freqs):
        whole = whole + lax.ppermute(sums, "freq", [(k, (k + step) % freqs) for k in range(freqs)])
    moments = jnp.sum(whole, axis=1)
    gamma, delta = moments[0], moments[1]
    alpha = gamma / delta
    gamma_new = gamma - 2.0 * alpha * moments[2] + alpha * alpha * moments[3]
    grow = 1.0 + gamma_new / gamma
    delta_new = grow * grow * delta - 2.0 * alpha * grow * moments[4] + alpha * alpha * moments[5]
    alpha_new = gamma_new / delta_new
    first = alpha + alpha_new * grow
    second = alpha * alpha_new

    def expand(x, c):
        return jnp.einsum("drb,drt->dbt", x.astype(jnp.float32), c, precision=HIGH).reshape(
            1, tile_dev * width, traces
        )

    model = expand(v, first * a0 - second * a1)
    gradient = expand(v, a0 - first * a1 + second * a2)
    residual = recorded - expand(u, first * b0 - second * b1)
    return model, residual, gradient


def solution(mesh):
    placed = (
        P("freq", "tile", None, None, None),
        P("freq", None, "tile", None, None),
        P("freq", None, None),
        P("freq", "tile", None),
    )
    out = P("freq", "tile", None)
    return jax.shard_map(local, mesh=mesh, in_specs=placed, out_specs=(out, out, out), check_vma=False)
```

```python
import functools

import jax
import jax.numpy as jnp
from jax import lax
from jax.experimental import pallas as pl
from jax.experimental.pallas import tpu as pltpu
from jax.sharding import PartitionSpec as P

HIGH = lax.Precision.HIGHEST
F32 = jnp.float32
BF16 = jnp.bfloat16
KERNEL_ROWS = 640
CHUNKS = 4


def vmem():
    return pl.BlockSpec(memory_space=pltpu.VMEM)


def smem():
    return pl.BlockSpec(memory_space=pltpu.SMEM)


def hbm():
    return pl.BlockSpec(memory_space=pltpu.HBM)


def params():
    return pltpu.CompilerParams(vmem_limit_bytes=12 * 1024 * 1024)


def masked(value, rank):
    level = lax.broadcasted_iota(jnp.int32, value.shape, 0)
    return jnp.where(level < rank, value, 0.0)


def start_kernel(tiles, rank_pad, ranks, u_hbm, field_hbm, out, u_buf, field_buf, sems):
    width = u_buf.shape[1]
    step = width // CHUNKS
    copies = []
    for c in range(CHUNKS):
        part = pl.ds(c * step, step)
        first = pltpu.make_async_copy(u_hbm.at[:, part], u_buf.at[:, part], sems.at[0, c])
        second = pltpu.make_async_copy(field_hbm.at[part], field_buf.at[part], sems.at[1, c])
        first.start()
        second.start()
        copies.append((first, second))
    total = jnp.zeros(out.shape, F32)
    for c, (first, second) in enumerate(copies):
        first.wait()
        second.wait()
        part = slice(c * step, (c + 1) * step)
        total += jnp.dot(u_buf[:, part], field_buf[part].astype(BF16), preferred_element_type=F32)
    for j in range(tiles):
        rows = slice(j * rank_pad, (j + 1) * rank_pad)
        out[rows] = masked(total[rows], ranks[j])


def start(u, field, ranks, tiles, rank_pad):
    rows, width = u.shape
    return pl.pallas_call(
        functools.partial(start_kernel, tiles, rank_pad),
        out_shape=jax.ShapeDtypeStruct((rows, field.shape[1]), F32),
        in_specs=[smem(), hbm(), hbm()],
        out_specs=vmem(),
        scratch_shapes=[
            pltpu.VMEM(u.shape, BF16),
            pltpu.VMEM(field.shape, F32),
            pltpu.SemaphoreType.DMA((2, CHUNKS)),
        ],
        cost_estimate=pl.CostEstimate(flops=2 * rows * width * 128, bytes_accessed=1200000, transcendentals=0),
        name="start",
    )(ranks, u, field)


def gram_kernel(tiles, rank_pad, ranks, x, high, low):
    g = lax.dot_general(x[...], x[...], (((1,), (1,)), ((), ())), preferred_element_type=F32)
    g = jnp.concatenate(
        [masked(g[k * rank_pad : (k + 1) * rank_pad], ranks[k]) for k in range(tiles)], axis=0
    )
    top = g.astype(BF16)
    high[...] = top
    low[...] = (g - top.astype(F32)).astype(BF16)


def gram(x, ranks, tiles, rank_pad):
    rows, width = x.shape
    out = jax.ShapeDtypeStruct((rows, rows), BF16)
    return pl.pallas_call(
        functools.partial(gram_kernel, tiles, rank_pad),
        out_shape=(out, out),
        in_specs=[smem(), vmem()],
        out_specs=(vmem(), vmem()),
        compiler_params=params(),
        cost_estimate=pl.CostEstimate(flops=2 * rows * rows * width, bytes_accessed=1200000, transcendentals=0),
        name="gram",
    )(ranks, x)


def product(high, low, c):
    top = c.astype(BF16)
    rest = (c - top.astype(F32)).astype(BF16)
    main = jnp.dot(high[...], top, preferred_element_type=F32)
    main += jnp.dot(high[...], rest, preferred_element_type=F32)
    return main + jnp.dot(low[...], top, preferred_element_type=F32)


def moment(x, y):
    return jnp.sum(x * y, axis=0, keepdims=True)


def step_kernel(high, low, c_ref, out, sums):
    c = c_ref[...]
    result = product(high, low, c)
    out[...] = result
    sums[...] = jnp.broadcast_to(moment(c, result), sums.shape)


def apply(halves, c):
    rows, traces = c.shape
    return pl.pallas_call(
        step_kernel,
        out_shape=(jax.ShapeDtypeStruct(c.shape, F32), jax.ShapeDtypeStruct((8, traces), F32)),
        in_specs=[vmem()] * 3,
        out_specs=(vmem(), vmem()),
        compiler_params=params(),
        cost_estimate=pl.CostEstimate(flops=6 * rows * rows * traces, bytes_accessed=700000, transcendentals=0),
        name="apply",
    )(*halves, c)


def last_kernel(tiles, rank_pad, high, low, c_ref, m0, m1, m2, out):
    c = c_ref[...]
    result = product(high, low, c)
    row = lax.broadcasted_iota(jnp.int32, m0.shape, 0)
    extra = jnp.where(row == 0, m0[...], 0.0)
    extra = jnp.where(row == 1, m1[...], extra)
    extra = jnp.where(row == 2, m2[...], extra)
    extra = jnp.where(row == 3, moment(c, result), extra)
    for j in range(tiles):
        out[j, :rank_pad] = result[j * rank_pad : (j + 1) * rank_pad]
        out[j, rank_pad:] = extra


def last(halves, c, sums, tiles, rank_pad):
    rows, traces = c.shape
    return pl.pallas_call(
        functools.partial(last_kernel, tiles, rank_pad),
        out_shape=jax.ShapeDtypeStruct((tiles, rank_pad + 8, traces), F32),
        in_specs=[vmem()] * 6,
        out_specs=vmem(),
        compiler_params=params(),
        cost_estimate=pl.CostEstimate(flops=6 * rows * rows * traces, bytes_accessed=700000, transcendentals=0),
        name="last",
    )(*halves, c, *sums)


def finish_kernel(
    tiles, rank_pad, s0, s1, s2, s3, a0, a1, packed, b0, b1, vt, ut, field, model_hbm, resid_hbm, grad_hbm, bufs, sems
):
    sums = s0[...] + s1[...] + s2[...] + s3[...]
    sums = jnp.sum(sums, axis=1, keepdims=True)
    m0, m1, m2, m3 = (sums[k : k + 1] for k in range(4))
    alpha = m0 / m1
    gamma = m0 - 2.0 * alpha * m1 + alpha * alpha * m2
    grow = 1.0 + gamma / m0
    delta = grow * grow * m1 - 2.0 * alpha * grow * m2 + alpha * alpha * m3
    alpha_new = gamma / delta
    first = alpha + alpha_new * grow
    second = alpha * alpha_new
    a2 = jnp.concatenate([packed[i, :rank_pad] for i in range(tiles)], axis=0)
    to_model = (first * a0[...] - second * a1[...]).astype(BF16)
    to_grad = (a0[...] - first * a1[...] + second * a2).astype(BF16)
    to_resid = (first * b0[...] - second * b1[...]).astype(BF16)
    step = field.shape[0] // CHUNKS
    copies = []
    for c in range(CHUNKS):
        part = slice(c * step, (c + 1) * step)
        where = pl.ds(c * step, step)
        bufs[0, part] = jnp.dot(vt[part], to_model, preferred_element_type=F32)
        bufs[1, part] = field[part] - jnp.dot(ut[part], to_resid, preferred_element_type=F32)
        bufs[2, part] = jnp.dot(vt[part], to_grad, preferred_element_type=F32)
        for k, out in enumerate((model_hbm, resid_hbm, grad_hbm)):
            copy = pltpu.make_async_copy(bufs.at[k, where], out.at[where], sems.at[k, c])
            copy.start()
            copies.append(copy)
    for copy in copies:
        copy.wait()


def finish(sums, a0, a1, packed, b0, b1, vt, ut, field, tiles, rank_pad):
    out = jax.ShapeDtypeStruct(field.shape, F32)
    return pl.pallas_call(
        functools.partial(finish_kernel, tiles, rank_pad),
        out_shape=(out, out, out),
        in_specs=[vmem()] * 12,
        out_specs=(hbm(), hbm(), hbm()),
        scratch_shapes=[pltpu.VMEM((3, *field.shape), F32), pltpu.SemaphoreType.DMA((3, CHUNKS))],
        compiler_params=params(),
        cost_estimate=pl.CostEstimate(flops=250000000, bytes_accessed=3000000, transcendentals=0),
        name="finish",
    )(*sums, a0, a1, packed, b0, b1, vt, ut, field)


def by_kernels(u_tiles, v_tiles, tile_ranks, recorded):
    _, _, tiles, rank_pad, width = u_tiles.shape
    traces = recorded.shape[2]
    freqs = lax.axis_size("freq")
    position = lax.axis_index("tile")
    rank_rows = lax.dynamic_slice_in_dim(tile_ranks[0], position, 1, 0).reshape(tiles)
    rank_cols = lax.dynamic_slice_in_dim(tile_ranks[0], position, 1, 1).reshape(tiles)
    u = u_tiles.reshape(tiles * rank_pad, width)
    v = v_tiles.reshape(tiles * rank_pad, width)
    field = recorded[0]

    def swap(c):
        c = c.reshape(tiles, -1, traces)
        return lax.all_to_all(c, "tile", split_axis=0, concat_axis=0, tiled=True)

    def flat(c):
        return c.reshape(tiles * rank_pad, traces)

    gram_v = gram(v, rank_cols, tiles, rank_pad)
    gram_u = gram(u, rank_rows, tiles, rank_pad)
    a0 = flat(swap(start(u, field, rank_rows, tiles, rank_pad)))
    a0, gram_v, gram_u, vt, ut = lax.optimization_barrier((a0, gram_v, gram_u, v.T, u.T))
    b0, m0 = apply(gram_v, a0)
    b0 = flat(swap(b0))
    a1, m1 = apply(gram_u, b0)
    a1 = flat(swap(a1))
    b1, m2 = apply(gram_v, a1)
    b1 = flat(swap(b1))
    packed = swap(last(gram_u, b1, (m0, m1, m2), tiles, rank_pad))
    sums = jnp.sum(packed[:, rank_pad:], axis=0)
    whole = [sums]
    for step in range(1, 4):
        whole.append(lax.ppermute(sums, "freq", [(k, k ^ step) for k in range(freqs)]))
    model, residual, gradient = finish(whole, a0, a1, packed, b0, b1, vt, ut, field, tiles, rank_pad)
    return model[None], residual[None], gradient[None]


def by_arrays(u_tiles, v_tiles, tile_ranks, recorded):
    _, tile_dev, tiles, rank_pad, width = u_tiles.shape
    traces = recorded.shape[2]
    freqs = lax.axis_size("freq")
    position = lax.axis_index("tile")
    levels = jnp.arange(rank_pad, dtype=jnp.int32)
    rank_rows = lax.dynamic_slice_in_dim(tile_ranks[0], position * tile_dev, tile_dev, 0)
    rank_cols = lax.dynamic_slice_in_dim(tile_ranks[0], position * tile_dev, tile_dev, 1)
    mask_rows = (levels < rank_rows[..., None]).astype(F32)
    mask_cols = (levels < rank_cols.T[..., None]).astype(F32)
    u = u_tiles[0].reshape(tile_dev, tiles * rank_pad, width)
    v = jnp.swapaxes(v_tiles[0], 0, 1).reshape(tile_dev, tiles * rank_pad, width)
    mask_u = mask_rows.reshape(tile_dev, tiles * rank_pad, 1)
    mask_v = mask_cols.reshape(tile_dev, tiles * rank_pad, 1)

    def gram_of(x):
        return jnp.einsum("drb,dsb->drs", x, x, preferred_element_type=F32)

    def swap(c):
        c = c.reshape(tile_dev, tiles, rank_pad, traces)
        c = lax.all_to_all(c, "tile", split_axis=1, concat_axis=0, tiled=True)
        return jnp.swapaxes(c, 0, 1).reshape(tile_dev, tiles * rank_pad, traces)

    def times(g, c, mask):
        return mask * jnp.einsum("drs,dst->drt", g, c, precision=HIGH)

    def dot(x, y):
        return jnp.sum(x * y)

    field = recorded.reshape(tile_dev, width, traces)
    gram_u, gram_v = gram_of(u), gram_of(v)
    a0 = swap(mask_u * jnp.einsum("drb,dbt->drt", u, field.astype(BF16), preferred_element_type=F32))
    b0v = times(gram_v, a0, mask_v)
    b0 = swap(b0v)
    a1u = times(gram_u, b0, mask_u)
    a1 = swap(a1u)
    b1v = times(gram_v, a1, mask_v)
    b1 = swap(b1v)
    a2u = times(gram_u, b1, mask_u)
    a2 = swap(a2u)
    parts = jnp.stack([dot(a0, b0v), dot(b0, a1u), dot(a1, b1v), dot(b1, a2u)])
    m0, m1, m2, m3 = lax.psum(lax.psum(parts, "tile"), "freq")
    alpha = m0 / m1
    gamma = m0 - 2.0 * alpha * m1 + alpha * alpha * m2
    grow = 1.0 + gamma / m0
    delta = grow * grow * m1 - 2.0 * alpha * grow * m2 + alpha * alpha * m3
    alpha_new = gamma / delta
    first = alpha + alpha_new * grow
    second = alpha * alpha_new

    def expand(x, c):
        image = jnp.einsum("drb,drt->dbt", x.astype(F32), c, precision=HIGH)
        return image.reshape(1, tile_dev * width, traces)

    model = expand(v, first * a0 - second * a1)
    gradient = expand(v, a0 - first * a1 + second * a2)
    residual = recorded - expand(u, first * b0 - second * b1)
    return model, residual, gradient


def local(u_tiles, v_tiles, tile_ranks, recorded):
    _, tile_dev, tiles, rank_pad, _ = u_tiles.shape
    small = tile_dev == 1 and tiles * rank_pad <= KERNEL_ROWS and lax.axis_size("freq") == 4
    return (by_kernels if small else by_arrays)(u_tiles, v_tiles, tile_ranks, recorded)


def solution(mesh):
    placed = (
        P("freq", "tile", None, None, None),
        P("freq", None, "tile", None, None),
        P("freq", None, None),
        P("freq", "tile", None),
    )
    out = P("freq", "tile", None)
    return jax.shard_map(local, mesh=mesh, in_specs=placed, out_specs=(out, out, out), check_vma=False)
```

```python
import functools

import jax
import jax.numpy as jnp
from jax import lax
from jax.experimental import pallas as pl
from jax.experimental.pallas import tpu as pltpu
from jax.sharding import PartitionSpec as P

HIGH = lax.Precision.HIGHEST
F32 = jnp.float32
BF16 = jnp.bfloat16
KERNEL_ROWS = 640
CHUNKS = 4


def vmem():
    return pl.BlockSpec(memory_space=pltpu.VMEM)


def smem():
    return pl.BlockSpec(memory_space=pltpu.SMEM)


def hbm():
    return pl.BlockSpec(memory_space=pltpu.HBM)


def params():
    return pltpu.CompilerParams(vmem_limit_bytes=12 * 1024 * 1024)


def masked(value, rank):
    level = lax.broadcasted_iota(jnp.int32, value.shape, 0)
    return jnp.where(level < rank, value, 0.0)


def gram_kernel(tiles, rank_pad, by_row, ranks, x, high, low, kept):
    position = lax.axis_index("tile")
    for k in range(tiles):
        rank = ranks[position, k] if by_row else ranks[k, position]
        rows = slice(k * rank_pad, (k + 1) * rank_pad)
        kept[rows] = masked(x[rows].astype(F32), rank).astype(BF16)
    x = kept[...]
    g = lax.dot_general(x, x, (((1,), (1,)), ((), ())), preferred_element_type=F32)
    top = g.astype(BF16)
    high[...] = top
    low[...] = (g - top.astype(F32)).astype(BF16)


def gram(x, ranks, by_row, tiles, rank_pad):
    rows, width = x.shape
    out = jax.ShapeDtypeStruct((rows, rows), BF16)
    return pl.pallas_call(
        functools.partial(gram_kernel, tiles, rank_pad, by_row),
        out_shape=(out, out, jax.ShapeDtypeStruct(x.shape, BF16)),
        in_specs=[smem(), vmem()],
        out_specs=(vmem(), vmem(), vmem()),
        compiler_params=params(),
        cost_estimate=pl.CostEstimate(flops=2 * rows * rows * width, bytes_accessed=1200000, transcendentals=0),
        name="gram",
    )(ranks, x)


def product(high, low, c):
    if c.dtype == BF16:
        both = jnp.dot(high[...], c, preferred_element_type=F32)
        return both + jnp.dot(low[...], c, preferred_element_type=F32)
    top = c.astype(BF16)
    rest = (c - top.astype(F32)).astype(BF16)
    main = jnp.dot(high[...], top, preferred_element_type=F32)
    main += jnp.dot(high[...], rest, preferred_element_type=F32)
    return main + jnp.dot(low[...], top, preferred_element_type=F32)


def moment(x, y):
    return jnp.sum(x.astype(F32) * y, axis=0, keepdims=True)


def step_kernel(high, low, c_ref, out, sums):
    c = c_ref[...]
    result = product(high, low, c)
    out[...] = result
    sums[...] = jnp.broadcast_to(moment(c, result), sums.shape)


def apply(halves, c):
    rows, traces = c.shape
    return pl.pallas_call(
        step_kernel,
        out_shape=(jax.ShapeDtypeStruct(c.shape, F32), jax.ShapeDtypeStruct((8, traces), F32)),
        in_specs=[vmem()] * 3,
        out_specs=(vmem(), vmem()),
        compiler_params=params(),
        cost_estimate=pl.CostEstimate(flops=6 * rows * rows * traces, bytes_accessed=700000, transcendentals=0),
        name="apply",
    )(*halves, c)


def last_kernel(tiles, rank_pad, high, low, c_ref, m0, m1, m2, out):
    c = c_ref[...]
    result = product(high, low, c)
    row = lax.broadcasted_iota(jnp.int32, m0.shape, 0)
    extra = jnp.where(row == 0, m0[...], 0.0)
    extra = jnp.where(row == 1, m1[...], extra)
    extra = jnp.where(row == 2, m2[...], extra)
    extra = jnp.where(row == 3, moment(c, result), extra)
    for j in range(tiles):
        out[j, :rank_pad] = result[j * rank_pad : (j + 1) * rank_pad]
        out[j, rank_pad:] = extra


def last(halves, c, sums, tiles, rank_pad):
    rows, traces = c.shape
    return pl.pallas_call(
        functools.partial(last_kernel, tiles, rank_pad),
        out_shape=jax.ShapeDtypeStruct((tiles, rank_pad + 8, traces), F32),
        in_specs=[vmem()] * 6,
        out_specs=vmem(),
        compiler_params=params(),
        cost_estimate=pl.CostEstimate(flops=6 * rows * rows * traces, bytes_accessed=700000, transcendentals=0),
        name="last",
    )(*halves, c, *sums)


def finish_kernel(
    tiles, rank_pad, s0, s1, s2, s3, a0, a1, packed, b0, b1, vt, ut, field, model_hbm, resid_hbm, grad_hbm, bufs, sems
):
    sums = s0[...] + s1[...] + s2[...] + s3[...]
    sums = jnp.sum(sums, axis=1, keepdims=True)
    m0, m1, m2, m3 = (sums[k : k + 1] for k in range(4))
    alpha = m0 / m1
    gamma = m0 - 2.0 * alpha * m1 + alpha * alpha * m2
    grow = 1.0 + gamma / m0
    delta = grow * grow * m1 - 2.0 * alpha * grow * m2 + alpha * alpha * m3
    alpha_new = gamma / delta
    first = alpha + alpha_new * grow
    second = alpha * alpha_new
    a2 = jnp.concatenate([packed[i, :rank_pad] for i in range(tiles)], axis=0)
    to_model = (first * a0[...].astype(F32) - second * a1[...]).astype(BF16)
    to_grad = (a0[...].astype(F32) - first * a1[...] + second * a2).astype(BF16)
    to_resid = (first * b0[...] - second * b1[...]).astype(BF16)
    step = field.shape[0] // CHUNKS
    copies = []
    for c in range(CHUNKS):
        part = slice(c * step, (c + 1) * step)
        where = pl.ds(c * step, step)
        bufs[0, part] = jnp.dot(vt[part], to_model, preferred_element_type=F32)
        bufs[1, part] = field[part] - jnp.dot(ut[part], to_resid, preferred_element_type=F32)
        bufs[2, part] = jnp.dot(vt[part], to_grad, preferred_element_type=F32)
        for k, out in enumerate((model_hbm, resid_hbm, grad_hbm)):
            copy = pltpu.make_async_copy(bufs.at[k, where], out.at[where], sems.at[k, c])
            copy.start()
            copies.append(copy)
    for copy in copies:
        copy.wait()


def finish(sums, a0, a1, packed, b0, b1, vt, ut, field, tiles, rank_pad):
    out = jax.ShapeDtypeStruct(field.shape, F32)
    return pl.pallas_call(
        functools.partial(finish_kernel, tiles, rank_pad),
        out_shape=(out, out, out),
        in_specs=[vmem()] * 12,
        out_specs=(hbm(), hbm(), hbm()),
        scratch_shapes=[pltpu.VMEM((3, *field.shape), F32), pltpu.SemaphoreType.DMA((3, CHUNKS))],
        compiler_params=params(),
        cost_estimate=pl.CostEstimate(flops=250000000, bytes_accessed=3000000, transcendentals=0),
        name="finish",
    )(*sums, a0, a1, packed, b0, b1, vt, ut, field)


def by_kernels(u_tiles, v_tiles, tile_ranks, recorded):
    _, _, tiles, rank_pad, width = u_tiles.shape
    traces = recorded.shape[2]
    freqs = lax.axis_size("freq")
    u = u_tiles.reshape(tiles * rank_pad, width)
    v = v_tiles.reshape(tiles * rank_pad, width)
    field = recorded[0]

    def swap(c):
        c = c.reshape(tiles, -1, traces)
        return lax.all_to_all(c, "tile", split_axis=0, concat_axis=0, tiled=True)

    def flat(c):
        return c.reshape(tiles * rank_pad, traces)

    a0 = jnp.dot(u, field.astype(BF16), preferred_element_type=F32).astype(BF16)
    a0 = flat(swap(a0))
    high_u, low_u, kept_u = gram(u, tile_ranks[0], True, tiles, rank_pad)
    high_v, low_v, kept_v = gram(v, tile_ranks[0], False, tiles, rank_pad)
    a0, gram_v, gram_u, vt, ut = lax.optimization_barrier(
        (a0, (high_v, low_v), (high_u, low_u), kept_v.T, kept_u.T)
    )
    b0, m0 = apply(gram_v, a0)
    b0 = flat(swap(b0))
    a1, m1 = apply(gram_u, b0)
    a1 = flat(swap(a1))
    b1, m2 = apply(gram_v, a1)
    b1 = flat(swap(b1))
    packed = swap(last(gram_u, b1, (m0, m1, m2), tiles, rank_pad))
    sums = jnp.sum(packed[:, rank_pad:], axis=0)
    whole = [sums]
    for step in range(1, 4):
        whole.append(lax.ppermute(sums, "freq", [(k, k ^ step) for k in range(freqs)]))
    model, residual, gradient = finish(whole, a0, a1, packed, b0, b1, vt, ut, field, tiles, rank_pad)
    return model[None], residual[None], gradient[None]


def by_arrays(u_tiles, v_tiles, tile_ranks, recorded):
    _, tile_dev, tiles, rank_pad, width = u_tiles.shape
    traces = recorded.shape[2]
    freqs = lax.axis_size("freq")
    position = lax.axis_index("tile")
    levels = jnp.arange(rank_pad, dtype=jnp.int32)
    rank_rows = lax.dynamic_slice_in_dim(tile_ranks[0], position * tile_dev, tile_dev, 0)
    rank_cols = lax.dynamic_slice_in_dim(tile_ranks[0], position * tile_dev, tile_dev, 1)
    mask_rows = (levels < rank_rows[..., None]).astype(F32)
    mask_cols = (levels < rank_cols.T[..., None]).astype(F32)
    u = u_tiles[0].reshape(tile_dev, tiles * rank_pad, width)
    v = jnp.swapaxes(v_tiles[0], 0, 1).reshape(tile_dev, tiles * rank_pad, width)
    mask_u = mask_rows.reshape(tile_dev, tiles * rank_pad, 1)
    mask_v = mask_cols.reshape(tile_dev, tiles * rank_pad, 1)

    def gram_of(x):
        return jnp.einsum("drb,dsb->drs", x, x, preferred_element_type=F32)

    def swap(c):
        c = c.reshape(tile_dev, tiles, rank_pad, traces)
        c = lax.all_to_all(c, "tile", split_axis=1, concat_axis=0, tiled=True)
        return jnp.swapaxes(c, 0, 1).reshape(tile_dev, tiles * rank_pad, traces)

    def times(g, c, mask):
        return mask * jnp.einsum("drs,dst->drt", g, c, precision=HIGH)

    def dot(x, y):
        return jnp.sum(x * y)

    field = recorded.reshape(tile_dev, width, traces)
    gram_u, gram_v = gram_of(u), gram_of(v)
    a0 = swap(mask_u * jnp.einsum("drb,dbt->drt", u, field.astype(BF16), preferred_element_type=F32))
    b0v = times(gram_v, a0, mask_v)
    b0 = swap(b0v)
    a1u = times(gram_u, b0, mask_u)
    a1 = swap(a1u)
    b1v = times(gram_v, a1, mask_v)
    b1 = swap(b1v)
    a2u = times(gram_u, b1, mask_u)
    a2 = swap(a2u)
    parts = jnp.stack([dot(a0, b0v), dot(b0, a1u), dot(a1, b1v), dot(b1, a2u)])
    m0, m1, m2, m3 = lax.psum(lax.psum(parts, "tile"), "freq")
    alpha = m0 / m1
    gamma = m0 - 2.0 * alpha * m1 + alpha * alpha * m2
    grow = 1.0 + gamma / m0
    delta = grow * grow * m1 - 2.0 * alpha * grow * m2 + alpha * alpha * m3
    alpha_new = gamma / delta
    first = alpha + alpha_new * grow
    second = alpha * alpha_new

    def expand(x, c):
        image = jnp.einsum("drb,drt->dbt", x.astype(F32), c, precision=HIGH)
        return image.reshape(1, tile_dev * width, traces)

    model = expand(v, first * a0 - second * a1)
    gradient = expand(v, a0 - first * a1 + second * a2)
    residual = recorded - expand(u, first * b0 - second * b1)
    return model, residual, gradient


def local(u_tiles, v_tiles, tile_ranks, recorded):
    _, tile_dev, tiles, rank_pad, _ = u_tiles.shape
    small = tile_dev == 1 and tiles * rank_pad <= KERNEL_ROWS and lax.axis_size("freq") == 4
    return (by_kernels if small else by_arrays)(u_tiles, v_tiles, tile_ranks, recorded)


def solution(mesh):
    placed = (
        P("freq", "tile", None, None, None),
        P("freq", None, "tile", None, None),
        P("freq", None, None),
        P("freq", "tile", None),
    )
    out = P("freq", "tile", None)
    return jax.shard_map(local, mesh=mesh, in_specs=placed, out_specs=(out, out, out), check_vma=False)
```

```python
import functools

import jax
import jax.numpy as jnp
from jax import lax
from jax.experimental import pallas as pl
from jax.experimental.pallas import tpu as pltpu
from jax.sharding import PartitionSpec as P

HIGH = lax.Precision.HIGHEST
F32 = jnp.float32
BF16 = jnp.bfloat16
KERNEL_ROWS = 640
CHUNKS = 4


def vmem():
    return pl.BlockSpec(memory_space=pltpu.VMEM)


def smem():
    return pl.BlockSpec(memory_space=pltpu.SMEM)


def hbm():
    return pl.BlockSpec(memory_space=pltpu.HBM)


def params():
    return pltpu.CompilerParams(vmem_limit_bytes=12 * 1024 * 1024)


def setup_kernel(tiles, rank_pad, ranks, u_hbm, v_hbm, *refs):
    position = lax.axis_index("tile")
    bufs, sems = refs[6:]
    copies = [pltpu.make_async_copy(x, bufs.at[k], sems.at[k]) for k, x in enumerate((u_hbm, v_hbm))]
    for copy in copies:
        copy.start()
    for side, (high, low, mask_ref) in enumerate((refs[:3], refs[3:6])):
        level = lax.broadcasted_iota(jnp.int32, (rank_pad, mask_ref.shape[1]), 0)
        mask = jnp.concatenate(
            [
                jnp.where(level < (ranks[k, position] if side else ranks[position, k]), 1.0, 0.0)
                for k in range(tiles)
            ],
            axis=0,
        ).astype(BF16)
        mask_ref[...] = mask
        copies[side].wait()
        x = bufs[side] * jnp.concatenate([mask] * (bufs.shape[2] // mask.shape[1]), axis=1)
        g = lax.dot_general(x, x, (((1,), (1,)), ((), ())), preferred_element_type=F32)
        top = g.astype(BF16)
        high[...] = top
        low[...] = (g - top.astype(F32)).astype(BF16)


def setup(u, v, ranks, traces, tiles, rank_pad):
    rows, width = u.shape
    half = jax.ShapeDtypeStruct((rows, rows), BF16)
    mask = jax.ShapeDtypeStruct((rows, traces), BF16)
    return pl.pallas_call(
        functools.partial(setup_kernel, tiles, rank_pad),
        out_shape=(half, half, mask) * 2,
        in_specs=[smem(), hbm(), hbm()],
        out_specs=(vmem(),) * 6,
        scratch_shapes=[pltpu.VMEM((2, rows, width), BF16), pltpu.SemaphoreType.DMA((2,))],
        compiler_params=pltpu.CompilerParams(vmem_limit_bytes=54000 * 1024),
        cost_estimate=pl.CostEstimate(flops=4 * rows * rows * width, bytes_accessed=2400000, transcendentals=0),
        name="setup",
    )(ranks, u, v)


def product(high, low, c):
    top = c.astype(BF16)
    rest = (c - top.astype(F32)).astype(BF16)
    main = jnp.dot(high[...], top, preferred_element_type=F32)
    main += jnp.dot(high[...], rest, preferred_element_type=F32)
    return main + jnp.dot(low[...], top, preferred_element_type=F32)


def dot(x, y):
    return jnp.sum(x * y, axis=0, keepdims=True)


def send(c, known, out, rank_pad, extra=()):
    norm = dot(known, known)
    factor = jnp.where(norm > 0.0, dot(known, c) / jnp.where(norm > 0.0, norm, 1.0), 0.0)
    factor = factor.astype(BF16).astype(F32)
    rest = (c - factor * known).astype(BF16)
    spare = out.shape[1] - rank_pad
    row = lax.broadcasted_iota(jnp.int32, (spare, c.shape[1]), 0)
    tail = jnp.zeros(row.shape, F32)
    for k, value in enumerate((factor, *extra)):
        tail = jnp.where(row == k, value, tail)
    tail = tail.astype(BF16)
    for k in range(out.shape[0]):
        out[k, :rank_pad] = rest[k * rank_pad : (k + 1) * rank_pad]
        out[k, rank_pad:] = tail
    return rest.astype(F32) + factor * known


def receive(blocks, known, rank_pad):
    parts = []
    for k in range(blocks.shape[0]):
        factor = blocks[k, rank_pad:].astype(F32)[:1]
        parts.append(blocks[k, :rank_pad].astype(F32) + factor * known[k * rank_pad : (k + 1) * rank_pad])
    return jnp.concatenate(parts, axis=0)


def pieces(row):
    first = row.astype(BF16).astype(F32)
    second = (row - first).astype(BF16).astype(F32)
    return first, second, row - first - second


def fill(sums, row):
    sums[...] = jnp.broadcast_to(row, sums.shape)


def first_kernel(rank_pad, high, low, mask, a0_ref, out, b0_ref, kept, sums):
    a0 = a0_ref[...].astype(F32) * mask[...].astype(F32)
    kept[...] = a0
    b0 = product(high, low, a0)
    fill(sums, dot(a0, b0))
    b0_ref[...] = send(b0, a0, out, rank_pad)


def second_kernel(rank_pad, high, low, mask, a0_ref, blocks, out, a1_ref, b0_ref, sums):
    a0 = a0_ref[...].astype(F32) * mask[...].astype(F32)
    b0 = receive(blocks, a0, rank_pad)
    b0_ref[...] = b0
    a1 = product(high, low, b0)
    fill(sums, dot(b0, a1))
    a1_ref[...] = send(a1, a0, out, rank_pad)


def third_kernel(rank_pad, high, low, a0, b0, blocks, out, a1_ref, sums):
    a1 = receive(blocks, a0[...], rank_pad)
    a1_ref[...] = a1
    b1 = product(high, low, a1)
    fill(sums, dot(a1, b1))
    send(b1, b0[...], out, rank_pad)


def fourth_kernel(rank_pad, high, low, b0, a1, m0, m1, m2, blocks, out, b1_ref):
    b1 = receive(blocks, b0[...], rank_pad)
    b1_ref[...] = b1
    a2 = product(high, low, b1)
    sums = (m0[:1], m1[:1], m2[:1], dot(b1, a2))
    send(a2, a1[...], out, rank_pad, [part for row in sums for part in pieces(row)])


def step(kernel, rank_pad, spare, kept, name, *args):
    blocks = args[-1]
    tiles = args[0].shape[0] // rank_pad
    traces = blocks.shape[-1]
    rows = tiles * rank_pad
    shapes = [jax.ShapeDtypeStruct((tiles, rank_pad + spare, traces), BF16)]
    shapes += [jax.ShapeDtypeStruct((n, traces), F32) for n in kept]
    return pl.pallas_call(
        functools.partial(kernel, rank_pad),
        out_shape=tuple(shapes),
        in_specs=[vmem()] * len(args),
        out_specs=(vmem(),) * len(shapes),
        compiler_params=params(),
        cost_estimate=pl.CostEstimate(flops=6 * rows * rows * traces, bytes_accessed=900000, transcendentals=0),
        name=name,
    )(*args)


def finish_kernel(
    rank_pad, s0, s1, s2, s3, a0, a1, blocks, b0, b1, vt, ut, field, model_hbm, resid_hbm, grad_hbm, bufs, sems
):
    sums = s0[...] + s1[...] + s2[...] + s3[...]
    sums = jnp.sum(sums, axis=1, keepdims=True)
    m0, m1, m2, m3 = (sums[3 * k + 1 : 3 * k + 2] + sums[3 * k + 2 : 3 * k + 3] + sums[3 * k + 3 : 3 * k + 4] for k in range(4))
    alpha = m0 / m1
    gamma = m0 - 2.0 * alpha * m1 + alpha * alpha * m2
    grow = 1.0 + gamma / m0
    delta = grow * grow * m1 - 2.0 * alpha * grow * m2 + alpha * alpha * m3
    alpha_new = gamma / delta
    first = alpha + alpha_new * grow
    second = alpha * alpha_new
    a2 = receive(blocks, a1[...], rank_pad)
    to_model = (first * a0[...] - second * a1[...]).astype(BF16)
    to_grad = (a0[...] - first * a1[...] + second * a2).astype(BF16)
    to_resid = (first * b0[...] - second * b1[...]).astype(BF16)
    step_rows = field.shape[0] // CHUNKS
    copies = []
    for c in range(CHUNKS):
        part = slice(c * step_rows, (c + 1) * step_rows)
        where = pl.ds(c * step_rows, step_rows)
        bufs[0, part] = jnp.dot(vt[part], to_model, preferred_element_type=F32)
        bufs[1, part] = field[part] - jnp.dot(ut[part], to_resid, preferred_element_type=F32)
        bufs[2, part] = jnp.dot(vt[part], to_grad, preferred_element_type=F32)
        for k, out in enumerate((model_hbm, resid_hbm, grad_hbm)):
            copy = pltpu.make_async_copy(bufs.at[k, where], out.at[where], sems.at[k, c])
            copy.start()
            copies.append(copy)
    for copy in copies:
        copy.wait()


def finish(sums, a0, a1, blocks, b0, b1, vt, ut, field, rank_pad):
    out = jax.ShapeDtypeStruct(field.shape, F32)
    return pl.pallas_call(
        functools.partial(finish_kernel, rank_pad),
        out_shape=(out, out, out),
        in_specs=[vmem()] * 12,
        out_specs=(hbm(), hbm(), hbm()),
        scratch_shapes=[pltpu.VMEM((3, *field.shape), F32), pltpu.SemaphoreType.DMA((3, CHUNKS))],
        compiler_params=params(),
        cost_estimate=pl.CostEstimate(flops=250000000, bytes_accessed=3000000, transcendentals=0),
        name="finish",
    )(*sums, a0, a1, blocks, b0, b1, vt, ut, field)


def by_kernels(u_tiles, v_tiles, tile_ranks, recorded):
    _, _, tiles, rank_pad, width = u_tiles.shape
    traces = recorded.shape[2]
    freqs = lax.axis_size("freq")
    rows = tiles * rank_pad
    u = u_tiles.reshape(rows, width)
    v = v_tiles.reshape(rows, width)
    field = recorded[0]

    def swap(blocks):
        return lax.all_to_all(blocks, "tile", split_axis=0, concat_axis=0, tiled=True)

    mine = jnp.dot(u, field.astype(BF16), preferred_element_type=F32).astype(BF16)
    a0 = swap(mine.reshape(tiles, rank_pad, traces))
    ready = setup(u, v, tile_ranks[0], traces, tiles, rank_pad)
    a0, ready = lax.optimization_barrier((a0, ready))
    high_u, low_u, mask_u, high_v, low_v, mask_v = ready
    a0 = a0.reshape(rows, traces)
    out, b0_col, a0, m0 = step(first_kernel, rank_pad, 8, (rows, rows, 8), "first", high_v, low_v, mask_v, a0)
    out, a1_row, b0, m1 = step(
        second_kernel, rank_pad, 8, (rows, rows, 8), "second", high_u, low_u, mask_u, mine, swap(out)
    )
    out, a1, m2 = step(third_kernel, rank_pad, 8, (rows, 8), "third", high_v, low_v, a0, b0_col, swap(out))
    out, b1 = step(fourth_kernel, rank_pad, 16, (rows,), "fourth", high_u, low_u, b0, a1_row, m0, m1, m2, swap(out))
    blocks = swap(out)
    sums, u, v = lax.optimization_barrier((jnp.sum(blocks[:, rank_pad:].astype(F32), axis=0), u, v))
    whole = [sums]
    for shift in range(1, 4):
        whole.append(lax.ppermute(sums, "freq", [(k, k ^ shift) for k in range(freqs)]))
    model, residual, gradient = finish(whole, a0, a1, blocks, b0, b1, v.T, u.T, field, rank_pad)
    return model[None], residual[None], gradient[None]


def by_arrays(u_tiles, v_tiles, tile_ranks, recorded):
    _, tile_dev, tiles, rank_pad, width = u_tiles.shape
    traces = recorded.shape[2]
    freqs = lax.axis_size("freq")
    position = lax.axis_index("tile")
    levels = jnp.arange(rank_pad, dtype=jnp.int32)
    rank_rows = lax.dynamic_slice_in_dim(tile_ranks[0], position * tile_dev, tile_dev, 0)
    rank_cols = lax.dynamic_slice_in_dim(tile_ranks[0], position * tile_dev, tile_dev, 1)
    mask_rows = (levels < rank_rows[..., None]).astype(F32)
    mask_cols = (levels < rank_cols.T[..., None]).astype(F32)
    u = u_tiles[0].reshape(tile_dev, tiles * rank_pad, width)
    v = jnp.swapaxes(v_tiles[0], 0, 1).reshape(tile_dev, tiles * rank_pad, width)
    mask_u = mask_rows.reshape(tile_dev, tiles * rank_pad, 1)
    mask_v = mask_cols.reshape(tile_dev, tiles * rank_pad, 1)

    def gram_of(x):
        return jnp.einsum("drb,dsb->drs", x, x, preferred_element_type=F32)

    def swap(c):
        c = c.reshape(tile_dev, tiles, rank_pad, traces)
        c = lax.all_to_all(c, "tile", split_axis=1, concat_axis=0, tiled=True)
        return jnp.swapaxes(c, 0, 1).reshape(tile_dev, tiles * rank_pad, traces)

    def times(g, c, mask):
        return mask * jnp.einsum("drs,dst->drt", g, c, precision=HIGH)

    field = recorded.reshape(tile_dev, width, traces)
    gram_u, gram_v = gram_of(u), gram_of(v)
    a0 = swap(mask_u * jnp.einsum("drb,dbt->drt", u, field.astype(BF16), preferred_element_type=F32))
    b0v = times(gram_v, a0, mask_v)
    b0 = swap(b0v)
    a1u = times(gram_u, b0, mask_u)
    a1 = swap(a1u)
    b1v = times(gram_v, a1, mask_v)
    b1 = swap(b1v)
    a2u = times(gram_u, b1, mask_u)
    a2 = swap(a2u)
    parts = jnp.stack([jnp.sum(x * y) for x, y in ((a0, b0v), (b0, a1u), (a1, b1v), (b1, a2u))])
    m0, m1, m2, m3 = lax.psum(lax.psum(parts, "tile"), "freq")
    alpha = m0 / m1
    gamma = m0 - 2.0 * alpha * m1 + alpha * alpha * m2
    grow = 1.0 + gamma / m0
    delta = grow * grow * m1 - 2.0 * alpha * grow * m2 + alpha * alpha * m3
    alpha_new = gamma / delta
    first = alpha + alpha_new * grow
    second = alpha * alpha_new

    def expand(x, c):
        image = jnp.einsum("drb,drt->dbt", x.astype(F32), c, precision=HIGH)
        return image.reshape(1, tile_dev * width, traces)

    model = expand(v, first * a0 - second * a1)
    gradient = expand(v, a0 - first * a1 + second * a2)
    residual = recorded - expand(u, first * b0 - second * b1)
    return model, residual, gradient


def local(u_tiles, v_tiles, tile_ranks, recorded):
    _, tile_dev, tiles, rank_pad, _ = u_tiles.shape
    small = tile_dev == 1 and tiles * rank_pad <= KERNEL_ROWS and lax.axis_size("freq") == 4
    return (by_kernels if small else by_arrays)(u_tiles, v_tiles, tile_ranks, recorded)


def solution(mesh):
    placed = (
        P("freq", "tile", None, None, None),
        P("freq", None, "tile", None, None),
        P("freq", None, None),
        P("freq", "tile", None),
    )
    out = P("freq", "tile", None)
    return jax.shard_map(local, mesh=mesh, in_specs=placed, out_specs=(out, out, out), check_vma=False)
```

```python
import functools

import jax
import jax.numpy as jnp
from jax import lax
from jax.experimental import pallas as pl
from jax.experimental.pallas import tpu as pltpu
from jax.sharding import PartitionSpec as P

HIGH = lax.Precision.HIGHEST
F32 = jnp.float32
BF16 = jnp.bfloat16
KERNEL_ROWS = 640
CHUNKS = 4


def vmem():
    return pl.BlockSpec(memory_space=pltpu.VMEM)


def smem():
    return pl.BlockSpec(memory_space=pltpu.SMEM)


def hbm():
    return pl.BlockSpec(memory_space=pltpu.HBM)


def params():
    return pltpu.CompilerParams(vmem_limit_bytes=12 * 1024 * 1024)


def setup_kernel(tiles, rank_pad, ranks, mine_hbm, u_hbm, v_hbm, *refs):
    position = lax.axis_index("tile")
    mine, bufs, sems = refs[6:]
    copies = [pltpu.make_async_copy(x, bufs.at[k], sems.at[k]) for k, x in enumerate((u_hbm, v_hbm))]
    copies.append(pltpu.make_async_copy(mine_hbm, mine, sems.at[2]))
    for copy in copies:
        copy.start()
    for side, (high, low, mask_ref) in enumerate((refs[:3], refs[3:6])):
        level = lax.broadcasted_iota(jnp.int32, (rank_pad, mask_ref.shape[1]), 0)
        mask = jnp.concatenate(
            [
                jnp.where(level < (ranks[k, position] if side else ranks[position, k]), 1.0, 0.0)
                for k in range(tiles)
            ],
            axis=0,
        ).astype(BF16)
        if side:
            mask_ref[...] = mask
        else:
            copies[2].wait()
            mask_ref[...] = mine[...] * mask
        copies[side].wait()
        x = bufs[side] * jnp.concatenate([mask] * (bufs.shape[2] // mask.shape[1]), axis=1)
        g = lax.dot_general(x, x, (((1,), (1,)), ((), ())), preferred_element_type=F32)
        top = g.astype(BF16)
        high[...] = top
        low[...] = (g - top.astype(F32)).astype(BF16)


def setup(mine, u, v, ranks, tiles, rank_pad):
    rows, width = u.shape
    half = jax.ShapeDtypeStruct((rows, rows), BF16)
    mask = jax.ShapeDtypeStruct(mine.shape, BF16)
    return pl.pallas_call(
        functools.partial(setup_kernel, tiles, rank_pad),
        out_shape=(half, half, mask) * 2,
        in_specs=[smem(), hbm(), hbm(), hbm()],
        out_specs=(vmem(),) * 6,
        scratch_shapes=[
            pltpu.VMEM(mine.shape, BF16),
            pltpu.VMEM((2, rows, width), BF16),
            pltpu.SemaphoreType.DMA((3,)),
        ],
        compiler_params=pltpu.CompilerParams(vmem_limit_bytes=54000 * 1024),
        cost_estimate=pl.CostEstimate(flops=4 * rows * rows * width, bytes_accessed=2400000, transcendentals=0),
        name="setup",
    )(ranks, mine, u, v)


def product(high, low, c):
    top = c.astype(BF16)
    rest = (c - top.astype(F32)).astype(BF16)
    main = jnp.dot(high[...], top, preferred_element_type=F32)
    main += jnp.dot(high[...], rest, preferred_element_type=F32)
    return main + jnp.dot(low[...], top, preferred_element_type=F32)


def dot(x, y):
    return jnp.sum(x * y, axis=0, keepdims=True)


def send(c, known, out, rank_pad, extra=()):
    norm = dot(known, known)
    factor = jnp.where(norm > 0.0, dot(known, c) / jnp.where(norm > 0.0, norm, 1.0), 0.0)
    factor = factor.astype(BF16).astype(F32)
    rest = (c - factor * known).astype(BF16)
    spare = out.shape[1] - rank_pad
    row = lax.broadcasted_iota(jnp.int32, (spare, c.shape[1]), 0)
    tail = jnp.zeros(row.shape, F32)
    for k, value in enumerate((factor, *extra)):
        tail = jnp.where(row == k, value, tail)
    tail = tail.astype(BF16)
    for k in range(out.shape[0]):
        out[k, :rank_pad] = rest[k * rank_pad : (k + 1) * rank_pad]
        out[k, rank_pad:] = tail
    return rest.astype(F32) + factor * known


def receive(blocks, known, rank_pad):
    parts = []
    for k in range(blocks.shape[0]):
        factor = blocks[k, rank_pad:].astype(F32)[:1]
        parts.append(blocks[k, :rank_pad].astype(F32) + factor * known[k * rank_pad : (k + 1) * rank_pad])
    return jnp.concatenate(parts, axis=0)


def pieces(row):
    first = row.astype(BF16).astype(F32)
    second = (row - first).astype(BF16).astype(F32)
    return first, second, row - first - second


def fill(sums, row):
    sums[...] = jnp.broadcast_to(row, sums.shape)


def first_kernel(rank_pad, high, low, mask, a0_ref, out, b0_ref, kept, sums):
    a0 = a0_ref[...].astype(F32) * mask[...].astype(F32)
    kept[...] = a0
    b0 = product(high, low, a0)
    fill(sums, dot(a0, b0))
    b0_ref[...] = send(b0, a0, out, rank_pad)


def second_kernel(rank_pad, high, low, a0_ref, blocks, out, a1_ref, b0_ref, sums):
    a0 = a0_ref[...].astype(F32)
    b0 = receive(blocks, a0, rank_pad)
    b0_ref[...] = b0
    a1 = product(high, low, b0)
    fill(sums, dot(b0, a1))
    a1_ref[...] = send(a1, a0, out, rank_pad)


def third_kernel(rank_pad, high, low, a0, b0, blocks, out, a1_ref, sums):
    a1 = receive(blocks, a0[...], rank_pad)
    a1_ref[...] = a1
    b1 = product(high, low, a1)
    fill(sums, dot(a1, b1))
    send(b1, b0[...], out, rank_pad)


def fourth_kernel(rank_pad, high, low, b0, a1, m0, m1, m2, blocks, out, b1_ref):
    b1 = receive(blocks, b0[...], rank_pad)
    b1_ref[...] = b1
    a2 = product(high, low, b1)
    sums = (m0[:1], m1[:1], m2[:1], dot(b1, a2))
    send(a2, a1[...], out, rank_pad, [part for row in sums for part in pieces(row)])


def step(kernel, rank_pad, spare, kept, name, *args):
    blocks = args[-1]
    tiles = args[0].shape[0] // rank_pad
    traces = blocks.shape[-1]
    rows = tiles * rank_pad
    shapes = [jax.ShapeDtypeStruct((tiles, rank_pad + spare, traces), BF16)]
    shapes += [jax.ShapeDtypeStruct((n, traces), F32) for n in kept]
    return pl.pallas_call(
        functools.partial(kernel, rank_pad),
        out_shape=tuple(shapes),
        in_specs=[vmem()] * len(args),
        out_specs=(vmem(),) * len(shapes),
        compiler_params=params(),
        cost_estimate=pl.CostEstimate(flops=6 * rows * rows * traces, bytes_accessed=900000, transcendentals=0),
        name=name,
    )(*args)


def finish_kernel(
    rank_pad, s0, s1, s2, s3, a0, a1, blocks, b0, b1, vt, ut, field, model_hbm, resid_hbm, grad_hbm, bufs, sems
):
    sums = s0[...] + s1[...] + s2[...] + s3[...]
    sums = jnp.sum(sums, axis=1, keepdims=True)
    m0, m1, m2, m3 = (sums[3 * k + 1 : 3 * k + 2] + sums[3 * k + 2 : 3 * k + 3] + sums[3 * k + 3 : 3 * k + 4] for k in range(4))
    alpha = m0 / m1
    gamma = m0 - 2.0 * alpha * m1 + alpha * alpha * m2
    grow = 1.0 + gamma / m0
    delta = grow * grow * m1 - 2.0 * alpha * grow * m2 + alpha * alpha * m3
    alpha_new = gamma / delta
    first = alpha + alpha_new * grow
    second = alpha * alpha_new
    a2 = receive(blocks, a1[...], rank_pad)
    to_model = (first * a0[...] - second * a1[...]).astype(BF16)
    to_grad = (a0[...] - first * a1[...] + second * a2).astype(BF16)
    to_resid = (first * b0[...] - second * b1[...]).astype(BF16)
    step_rows = field.shape[0] // CHUNKS
    copies = []
    for c in range(CHUNKS):
        part = slice(c * step_rows, (c + 1) * step_rows)
        where = pl.ds(c * step_rows, step_rows)
        bufs[0, part] = jnp.dot(vt[part], to_model, preferred_element_type=F32)
        bufs[1, part] = field[part] - jnp.dot(ut[part], to_resid, preferred_element_type=F32)
        bufs[2, part] = jnp.dot(vt[part], to_grad, preferred_element_type=F32)
        for k, out in enumerate((model_hbm, resid_hbm, grad_hbm)):
            copy = pltpu.make_async_copy(bufs.at[k, where], out.at[where], sems.at[k, c])
            copy.start()
            copies.append(copy)
    for copy in copies:
        copy.wait()


def finish(sums, a0, a1, blocks, b0, b1, vt, ut, field, rank_pad):
    out = jax.ShapeDtypeStruct(field.shape, F32)
    return pl.pallas_call(
        functools.partial(finish_kernel, rank_pad),
        out_shape=(out, out, out),
        in_specs=[vmem()] * 12,
        out_specs=(hbm(), hbm(), hbm()),
        scratch_shapes=[pltpu.VMEM((3, *field.shape), F32), pltpu.SemaphoreType.DMA((3, CHUNKS))],
        compiler_params=params(),
        cost_estimate=pl.CostEstimate(flops=250000000, bytes_accessed=3000000, transcendentals=0),
        name="finish",
    )(*sums, a0, a1, blocks, b0, b1, vt, ut, field)


def by_kernels(u_tiles, v_tiles, tile_ranks, recorded):
    _, _, tiles, rank_pad, width = u_tiles.shape
    traces = recorded.shape[2]
    freqs = lax.axis_size("freq")
    rows = tiles * rank_pad
    u = u_tiles.reshape(rows, width)
    v = v_tiles.reshape(rows, width)
    field = recorded[0]

    def swap(blocks):
        return lax.all_to_all(blocks, "tile", split_axis=0, concat_axis=0, tiled=True)

    mine = jnp.dot(u, field.astype(BF16), preferred_element_type=F32).astype(BF16)
    a0 = swap(mine.reshape(tiles, rank_pad, traces))
    ready = setup(mine, u, v, tile_ranks[0], tiles, rank_pad)
    a0, ready = lax.optimization_barrier((a0, ready))
    high_u, low_u, mine, high_v, low_v, mask_v = ready
    a0 = a0.reshape(rows, traces)
    out, b0_col, a0, m0 = step(first_kernel, rank_pad, 8, (rows, rows, 8), "first", high_v, low_v, mask_v, a0)
    out, a1_row, b0, m1 = step(
        second_kernel, rank_pad, 8, (rows, rows, 8), "second", high_u, low_u, mine, swap(out)
    )
    out, a1, m2 = step(third_kernel, rank_pad, 8, (rows, 8), "third", high_v, low_v, a0, b0_col, swap(out))
    out, b1 = step(fourth_kernel, rank_pad, 16, (rows,), "fourth", high_u, low_u, b0, a1_row, m0, m1, m2, swap(out))
    blocks = swap(out)
    sums, u, v = lax.optimization_barrier((jnp.sum(blocks[:, rank_pad:].astype(F32), axis=0), u, v))
    whole = [sums]
    for shift in range(1, 4):
        whole.append(lax.ppermute(sums, "freq", [(k, k ^ shift) for k in range(freqs)]))
    model, residual, gradient = finish(whole, a0, a1, blocks, b0, b1, v.T, u.T, field, rank_pad)
    return model[None], residual[None], gradient[None]


def by_arrays(u_tiles, v_tiles, tile_ranks, recorded):
    _, tile_dev, tiles, rank_pad, width = u_tiles.shape
    traces = recorded.shape[2]
    freqs = lax.axis_size("freq")
    position = lax.axis_index("tile")
    levels = jnp.arange(rank_pad, dtype=jnp.int32)
    rank_rows = lax.dynamic_slice_in_dim(tile_ranks[0], position * tile_dev, tile_dev, 0)
    rank_cols = lax.dynamic_slice_in_dim(tile_ranks[0], position * tile_dev, tile_dev, 1)
    mask_rows = (levels < rank_rows[..., None]).astype(F32)
    mask_cols = (levels < rank_cols.T[..., None]).astype(F32)
    u = u_tiles[0].reshape(tile_dev, tiles * rank_pad, width)
    v = jnp.swapaxes(v_tiles[0], 0, 1).reshape(tile_dev, tiles * rank_pad, width)
    mask_u = mask_rows.reshape(tile_dev, tiles * rank_pad, 1)
    mask_v = mask_cols.reshape(tile_dev, tiles * rank_pad, 1)

    def gram_of(x):
        return jnp.einsum("drb,dsb->drs", x, x, preferred_element_type=F32)

    def swap(c):
        c = c.reshape(tile_dev, tiles, rank_pad, traces)
        c = lax.all_to_all(c, "tile", split_axis=1, concat_axis=0, tiled=True)
        return jnp.swapaxes(c, 0, 1).reshape(tile_dev, tiles * rank_pad, traces)

    def times(g, c, mask):
        return mask * jnp.einsum("drs,dst->drt", g, c, precision=HIGH)

    field = recorded.reshape(tile_dev, width, traces)
    gram_u, gram_v = gram_of(u), gram_of(v)
    a0 = swap(mask_u * jnp.einsum("drb,dbt->drt", u, field.astype(BF16), preferred_element_type=F32))
    b0v = times(gram_v, a0, mask_v)
    b0 = swap(b0v)
    a1u = times(gram_u, b0, mask_u)
    a1 = swap(a1u)
    b1v = times(gram_v, a1, mask_v)
    b1 = swap(b1v)
    a2u = times(gram_u, b1, mask_u)
    a2 = swap(a2u)
    parts = jnp.stack([jnp.sum(x * y) for x, y in ((a0, b0v), (b0, a1u), (a1, b1v), (b1, a2u))])
    m0, m1, m2, m3 = lax.psum(lax.psum(parts, "tile"), "freq")
    alpha = m0 / m1
    gamma = m0 - 2.0 * alpha * m1 + alpha * alpha * m2
    grow = 1.0 + gamma / m0
    delta = grow * grow * m1 - 2.0 * alpha * grow * m2 + alpha * alpha * m3
    alpha_new = gamma / delta
    first = alpha + alpha_new * grow
    second = alpha * alpha_new

    def expand(x, c):
        image = jnp.einsum("drb,drt->dbt", x.astype(F32), c, precision=HIGH)
        return image.reshape(1, tile_dev * width, traces)

    model = expand(v, first * a0 - second * a1)
    gradient = expand(v, a0 - first * a1 + second * a2)
    residual = recorded - expand(u, first * b0 - second * b1)
    return model, residual, gradient


def local(u_tiles, v_tiles, tile_ranks, recorded):
    _, tile_dev, tiles, rank_pad, _ = u_tiles.shape
    small = tile_dev == 1 and tiles * rank_pad <= KERNEL_ROWS and lax.axis_size("freq") == 4
    return (by_kernels if small else by_arrays)(u_tiles, v_tiles, tile_ranks, recorded)


def solution(mesh):
    placed = (
        P("freq", "tile", None, None, None),
        P("freq", None, "tile", None, None),
        P("freq", None, None),
        P("freq", "tile", None),
    )
    out = P("freq", "tile", None)
    return jax.shard_map(local, mesh=mesh, in_specs=placed, out_specs=(out, out, out), check_vma=False)
```

```python
import functools

import jax
import jax.numpy as jnp
from jax import lax
from jax.experimental import pallas as pl
from jax.experimental.pallas import tpu as pltpu
from jax.sharding import PartitionSpec as P

HIGH = lax.Precision.HIGHEST
F32 = jnp.float32
BF16 = jnp.bfloat16
KERNEL_ROWS = 640
CHUNKS = 4
BLOCK = 256


def vmem():
    return pl.BlockSpec(memory_space=pltpu.VMEM)


def hbm():
    return pl.BlockSpec(memory_space=pltpu.HBM)


def params():
    return pltpu.CompilerParams(vmem_limit_bytes=12 * 1024 * 1024)


def gram_columns(rows):
    return [(c, min(BLOCK, rows - c)) for c in range(0, rows, BLOCK)]


def gram_part(x):
    return [
        lax.dot_general(x[c:], x[c : c + n], (((1,), (1,)), ((), ())), preferred_element_type=F32)
        for c, n in gram_columns(x.shape[0])
    ]


def gram_store(parts, high, low):
    for (c, n), g in zip(gram_columns(high.shape[0]), parts):
        top = g.astype(BF16)
        rest = (g - top.astype(F32)).astype(BF16)
        high[c:, c : c + n] = top
        low[c:, c : c + n] = rest
        if g.shape[0] > n:
            above = g[n:].T
            top = above.astype(BF16)
            high[c : c + n, c + n :] = top
            low[c : c + n, c + n :] = (above - top.astype(F32)).astype(BF16)


def mask_of(rank, tiles, rank_pad, traces):
    level = lax.broadcasted_iota(jnp.int32, (rank_pad, traces), 0)
    return jnp.concatenate([jnp.where(level < rank(k), 1.0, 0.0) for k in range(tiles)], axis=0)


def prologue_kernel(u_hbm, field_hbm, out, high, low, u, field, sems):
    copies = [pltpu.make_async_copy(u_hbm, u, sems.at[0]), pltpu.make_async_copy(field_hbm, field, sems.at[1])]
    for copy in copies:
        copy.start()
    for copy in copies:
        copy.wait()
    out[...] = jnp.dot(u[...], field[...].astype(BF16), preferred_element_type=F32).astype(BF16)
    gram_store(gram_part(u[...]), high, low)


def prologue(u, field):
    rows, width = u.shape
    half = jax.ShapeDtypeStruct((rows, rows), BF16)
    return pl.pallas_call(
        prologue_kernel,
        out_shape=(jax.ShapeDtypeStruct((rows, field.shape[1]), BF16), half, half),
        in_specs=[hbm(), hbm()],
        out_specs=(vmem(),) * 3,
        scratch_shapes=[
            pltpu.VMEM(u.shape, BF16),
            pltpu.VMEM(field.shape, F32),
            pltpu.SemaphoreType.DMA((2,)),
        ],
        compiler_params=pltpu.CompilerParams(vmem_limit_bytes=54400 * 1024),
        cost_estimate=pl.CostEstimate(flops=4 * rows * rows * width, bytes_accessed=1200000, transcendentals=0),
        name="prologue",
    )(u, field)


def product(high, low, c):
    top = c.astype(BF16)
    rest = (c - top.astype(F32)).astype(BF16)
    n = c.shape[1]
    main = jnp.dot(high[...], jnp.concatenate([top, rest], axis=1), preferred_element_type=F32)
    return main[:, :n] + main[:, n:] + jnp.dot(low[...], top, preferred_element_type=F32)


def dot(x, y):
    return jnp.sum(x * y, axis=0, keepdims=True)


def send(c, known, out, rank_pad, extra=()):
    norm = dot(known, known)
    factor = jnp.where(norm > 0.0, dot(known, c) / jnp.where(norm > 0.0, norm, 1.0), 0.0)
    factor = factor.astype(BF16).astype(F32)
    rest = (c - factor * known).astype(BF16)
    spare = out.shape[1] - rank_pad
    row = lax.broadcasted_iota(jnp.int32, (spare, c.shape[1]), 0)
    tail = jnp.zeros(row.shape, F32)
    for k, value in enumerate((factor, *extra)):
        tail = jnp.where(row == k, value, tail)
    tail = tail.astype(BF16)
    for k in range(out.shape[0]):
        out[k, :rank_pad] = rest[k * rank_pad : (k + 1) * rank_pad]
        out[k, rank_pad:] = tail
    return rest.astype(F32) + factor * known


def receive(blocks, known, rank_pad):
    parts = []
    for k in range(blocks.shape[0]):
        factor = blocks[k, rank_pad:].astype(F32)[:1]
        parts.append(blocks[k, :rank_pad].astype(F32) + factor * known[k * rank_pad : (k + 1) * rank_pad])
    return jnp.concatenate(parts, axis=0)


def pieces(row):
    first = row.astype(BF16).astype(F32)
    second = (row - first).astype(BF16).astype(F32)
    return first, second, row - first - second


def fill(sums, row):
    sums[...] = jnp.broadcast_to(row, sums.shape)


def first_kernel(rank_pad, ranks, v, a0_ref, out, high, low, mask_u, mask_v, b0_ref, kept, sums):
    tiles, traces = out.shape[0], out.shape[2]
    position = lax.axis_index("tile")
    table = ranks[...]
    row = jnp.sum(jnp.where(lax.broadcasted_iota(jnp.int32, table.shape, 0) == position, table, 0), axis=0, keepdims=True)
    col = jnp.sum(jnp.where(lax.broadcasted_iota(jnp.int32, table.shape, 1) == position, table, 0), axis=1, keepdims=True)
    mask_u[...] = mask_of(lambda k: row[:, k : k + 1], tiles, rank_pad, traces)
    mask = mask_of(lambda k: col[k : k + 1], tiles, rank_pad, traces)
    mask_v[...] = mask
    a0 = a0_ref[...].astype(F32) * mask
    kept[...] = a0
    gram_store(gram_part(v[...]), high, low)
    b0 = product(high, low, a0) * mask
    fill(sums, dot(a0, b0))
    b0_ref[...] = send(b0, a0, out, rank_pad)


def second_kernel(rank_pad, high, low, mask, a0_ref, blocks, out, a1_ref, b0_ref, sums):
    a0 = a0_ref[...].astype(F32) * mask[...]
    b0 = receive(blocks, a0, rank_pad)
    b0_ref[...] = b0
    a1 = product(high, low, b0) * mask[...]
    fill(sums, dot(b0, a1))
    a1_ref[...] = send(a1, a0, out, rank_pad)


def third_kernel(rank_pad, high, low, mask, a0, b0, blocks, out, a1_ref, sums):
    a1 = receive(blocks, a0[...], rank_pad)
    a1_ref[...] = a1
    b1 = product(high, low, a1) * mask[...]
    fill(sums, dot(a1, b1))
    send(b1, b0[...], out, rank_pad)


def fourth_kernel(rank_pad, high, low, mask, b0, a1, m0, m1, m2, blocks, out, b1_ref):
    b1 = receive(blocks, b0[...], rank_pad)
    b1_ref[...] = b1
    a2 = product(high, low, b1) * mask[...]
    sums = (m0[:1], m1[:1], m2[:1], dot(b1, a2))
    send(a2, a1[...], out, rank_pad, [part for row in sums for part in pieces(row)])


def step(kernel, tiles, rank_pad, spare, kept, name, *args):
    traces = args[-1].shape[-1]
    rows = tiles * rank_pad
    shapes = [jax.ShapeDtypeStruct((tiles, rank_pad + spare, traces), BF16)]
    shapes += [jax.ShapeDtypeStruct(*shape) for shape in kept]
    return pl.pallas_call(
        functools.partial(kernel, rank_pad),
        out_shape=tuple(shapes),
        in_specs=[vmem()] * len(args),
        out_specs=(vmem(),) * len(shapes),
        compiler_params=params(),
        cost_estimate=pl.CostEstimate(flops=6 * rows * rows * traces, bytes_accessed=900000, transcendentals=0),
        name=name,
    )(*args)


def finish_kernel(
    rank_pad, s0, s1, s2, s3, a0, a1, blocks, b0, b1, vt, ut, field, model_hbm, resid_hbm, grad_hbm, bufs, sems
):
    sums = s0[...] + s1[...] + s2[...] + s3[...]
    sums = jnp.sum(sums, axis=1, keepdims=True)
    m0, m1, m2, m3 = (sums[3 * k + 1 : 3 * k + 2] + sums[3 * k + 2 : 3 * k + 3] + sums[3 * k + 3 : 3 * k + 4] for k in range(4))
    alpha = m0 / m1
    gamma = m0 - 2.0 * alpha * m1 + alpha * alpha * m2
    grow = 1.0 + gamma / m0
    delta = grow * grow * m1 - 2.0 * alpha * grow * m2 + alpha * alpha * m3
    alpha_new = gamma / delta
    first = alpha + alpha_new * grow
    second = alpha * alpha_new
    a2 = receive(blocks, a1[...], rank_pad)
    to_model = (first * a0[...] - second * a1[...]).astype(BF16)
    to_grad = (a0[...] - first * a1[...] + second * a2).astype(BF16)
    to_resid = (first * b0[...] - second * b1[...]).astype(BF16)
    to_both = jnp.concatenate([to_model, to_grad], axis=1)
    step_rows = field.shape[0] // CHUNKS
    copies = []
    for c in range(CHUNKS):
        part = slice(c * step_rows, (c + 1) * step_rows)
        where = pl.ds(c * step_rows, step_rows)
        both = jnp.dot(vt[part], to_both, preferred_element_type=F32)
        bufs[0, part] = both[:, : both.shape[1] // 2]
        bufs[2, part] = both[:, both.shape[1] // 2 :]
        bufs[1, part] = field[part] - jnp.dot(ut[part], to_resid, preferred_element_type=F32)
        for k, out in enumerate((model_hbm, resid_hbm, grad_hbm)):
            copy = pltpu.make_async_copy(bufs.at[k, where], out.at[where], sems.at[k, c])
            copy.start()
            copies.append(copy)
    for copy in copies:
        copy.wait()


def finish(sums, a0, a1, blocks, b0, b1, vt, ut, field, rank_pad):
    out = jax.ShapeDtypeStruct(field.shape, F32)
    return pl.pallas_call(
        functools.partial(finish_kernel, rank_pad),
        out_shape=(out, out, out),
        in_specs=[vmem()] * 12,
        out_specs=(hbm(), hbm(), hbm()),
        scratch_shapes=[pltpu.VMEM((3, *field.shape), F32), pltpu.SemaphoreType.DMA((3, CHUNKS))],
        compiler_params=params(),
        cost_estimate=pl.CostEstimate(flops=250000000, bytes_accessed=3000000, transcendentals=0),
        name="finish",
    )(*sums, a0, a1, blocks, b0, b1, vt, ut, field)


def by_kernels(u_tiles, v_tiles, tile_ranks, recorded):
    _, _, tiles, rank_pad, width = u_tiles.shape
    traces = recorded.shape[2]
    freqs = lax.axis_size("freq")
    rows = tiles * rank_pad
    u = u_tiles.reshape(rows, width)
    v = v_tiles.reshape(rows, width)
    field = recorded[0]

    def swap(blocks):
        return lax.all_to_all(blocks, "tile", split_axis=0, concat_axis=0, tiled=True)

    mine, high_u, low_u = prologue(u, field)
    mine, v = lax.optimization_barrier((mine, v))
    a0 = swap(mine.reshape(tiles, rank_pad, traces)).reshape(rows, traces)
    wide, short, half = ((rows, traces), F32), ((8, traces), F32), ((rows, rows), BF16)
    out, high_v, low_v, mask_u, mask_v, b0_col, a0, m0 = step(
        first_kernel, tiles, rank_pad, 8, (half, half, wide, wide, wide, wide, short), "first", tile_ranks[0], v, a0
    )
    out, a1_row, b0, m1 = step(
        second_kernel, tiles, rank_pad, 8, (wide, wide, short), "second", high_u, low_u, mask_u, mine, swap(out)
    )
    out, a1, m2 = step(third_kernel, tiles, rank_pad, 8, (wide, short), "third", high_v, low_v, mask_v, a0, b0_col, swap(out))
    out, b1 = step(
        fourth_kernel, tiles, rank_pad, 16, (wide,), "fourth", high_u, low_u, mask_u, b0, a1_row, m0, m1, m2, swap(out)
    )
    blocks = swap(out)
    sums, u, v = lax.optimization_barrier((jnp.sum(blocks[:, rank_pad:].astype(F32), axis=0), u, v))
    whole = [sums]
    for shift in range(1, 4):
        whole.append(lax.ppermute(sums, "freq", [(k, k ^ shift) for k in range(freqs)]))
    model, residual, gradient = finish(whole, a0, a1, blocks, b0, b1, v.T, u.T, field, rank_pad)
    return model[None], residual[None], gradient[None]


def by_arrays(u_tiles, v_tiles, tile_ranks, recorded):
    _, tile_dev, tiles, rank_pad, width = u_tiles.shape
    traces = recorded.shape[2]
    freqs = lax.axis_size("freq")
    position = lax.axis_index("tile")
    levels = jnp.arange(rank_pad, dtype=jnp.int32)
    rank_rows = lax.dynamic_slice_in_dim(tile_ranks[0], position * tile_dev, tile_dev, 0)
    rank_cols = lax.dynamic_slice_in_dim(tile_ranks[0], position * tile_dev, tile_dev, 1)
    mask_rows = (levels < rank_rows[..., None]).astype(F32)
    mask_cols = (levels < rank_cols.T[..., None]).astype(F32)
    u = u_tiles[0].reshape(tile_dev, tiles * rank_pad, width)
    v = jnp.swapaxes(v_tiles[0], 0, 1).reshape(tile_dev, tiles * rank_pad, width)
    mask_u = mask_rows.reshape(tile_dev, tiles * rank_pad, 1)
    mask_v = mask_cols.reshape(tile_dev, tiles * rank_pad, 1)

    def gram_of(x):
        return jnp.einsum("drb,dsb->drs", x, x, preferred_element_type=F32)

    def swap(c):
        c = c.reshape(tile_dev, tiles, rank_pad, traces)
        c = lax.all_to_all(c, "tile", split_axis=1, concat_axis=0, tiled=True)
        return jnp.swapaxes(c, 0, 1).reshape(tile_dev, tiles * rank_pad, traces)

    def times(g, c, mask):
        return mask * jnp.einsum("drs,dst->drt", g, c, precision=HIGH)

    field = recorded.reshape(tile_dev, width, traces)
    gram_u, gram_v = gram_of(u), gram_of(v)
    a0 = swap(mask_u * jnp.einsum("drb,dbt->drt", u, field.astype(BF16), preferred_element_type=F32))
    b0v = times(gram_v, a0, mask_v)
    b0 = swap(b0v)
    a1u = times(gram_u, b0, mask_u)
    a1 = swap(a1u)
    b1v = times(gram_v, a1, mask_v)
    b1 = swap(b1v)
    a2u = times(gram_u, b1, mask_u)
    a2 = swap(a2u)
    parts = jnp.stack([jnp.sum(x * y) for x, y in ((a0, b0v), (b0, a1u), (a1, b1v), (b1, a2u))])
    m0, m1, m2, m3 = lax.psum(lax.psum(parts, "tile"), "freq")
    alpha = m0 / m1
    gamma = m0 - 2.0 * alpha * m1 + alpha * alpha * m2
    grow = 1.0 + gamma / m0
    delta = grow * grow * m1 - 2.0 * alpha * grow * m2 + alpha * alpha * m3
    alpha_new = gamma / delta
    first = alpha + alpha_new * grow
    second = alpha * alpha_new

    def expand(x, c):
        image = jnp.einsum("drb,drt->dbt", x.astype(F32), c, precision=HIGH)
        return image.reshape(1, tile_dev * width, traces)

    model = expand(v, first * a0 - second * a1)
    gradient = expand(v, a0 - first * a1 + second * a2)
    residual = recorded - expand(u, first * b0 - second * b1)
    return model, residual, gradient


def local(u_tiles, v_tiles, tile_ranks, recorded):
    _, tile_dev, tiles, rank_pad, _ = u_tiles.shape
    small = tile_dev == 1 and tiles * rank_pad <= KERNEL_ROWS and lax.axis_size("freq") == 4
    return (by_kernels if small else by_arrays)(u_tiles, v_tiles, tile_ranks, recorded)


def solution(mesh):
    placed = (
        P("freq", "tile", None, None, None),
        P("freq", None, "tile", None, None),
        P("freq", None, None),
        P("freq", "tile", None),
    )
    out = P("freq", "tile", None)
    return jax.shard_map(local, mesh=mesh, in_specs=placed, out_specs=(out, out, out), check_vma=False)
```

```python
import functools

import jax
import jax.numpy as jnp
from jax import lax
from jax.experimental import pallas as pl
from jax.experimental.pallas import tpu as pltpu
from jax.sharding import PartitionSpec as P

HIGH = lax.Precision.HIGHEST
F32 = jnp.float32
BF16 = jnp.bfloat16
KERNEL_ROWS = 640
CHUNKS = 4
BLOCK = 256


def vmem():
    return pl.BlockSpec(memory_space=pltpu.VMEM)


def hbm():
    return pl.BlockSpec(memory_space=pltpu.HBM)


def params():
    return pltpu.CompilerParams(vmem_limit_bytes=12 * 1024 * 1024)


def gram_columns(rows):
    return [(c, min(BLOCK, rows - c)) for c in range(0, rows, BLOCK)]


def gram_part(x):
    return [
        lax.dot_general(x[c:], x[c : c + n], (((1,), (1,)), ((), ())), preferred_element_type=F32)
        for c, n in gram_columns(x.shape[0])
    ]


def gram_store(parts, high, low):
    for (c, n), g in zip(gram_columns(high.shape[0]), parts):
        top = g.astype(BF16)
        rest = (g - top.astype(F32)).astype(BF16)
        high[c:, c : c + n] = top
        low[c:, c : c + n] = rest
        if g.shape[0] > n:
            above = g[n:].T
            top = above.astype(BF16)
            high[c : c + n, c + n :] = top
            low[c : c + n, c + n :] = (above - top.astype(F32)).astype(BF16)


def mask_of(rank, tiles, rank_pad, traces):
    level = lax.broadcasted_iota(jnp.int32, (rank_pad, traces), 0)
    return jnp.concatenate([jnp.where(level < rank(k), 1.0, 0.0) for k in range(tiles)], axis=0)


def prologue_kernel(u_hbm, field_hbm, out, kept, high, low, u, field, sems):
    copies = [pltpu.make_async_copy(u_hbm, u, sems.at[0]), pltpu.make_async_copy(field_hbm, field, sems.at[1])]
    for copy in copies:
        copy.start()
    for copy in copies:
        copy.wait()
    mine = jnp.dot(u[...], field[...].astype(BF16), preferred_element_type=F32)
    kept[...] = mine.astype(BF16)
    pack(mine, out, [jnp.max(jnp.abs(mine), axis=0, keepdims=True)])
    gram_store(gram_part(u[...]), high, low)


def prologue(u, field, tiles, rank_pad):
    rows, width = u.shape
    traces = field.shape[1]
    half = jax.ShapeDtypeStruct((rows, rows), BF16)
    return pl.pallas_call(
        prologue_kernel,
        out_shape=(
            jax.ShapeDtypeStruct((tiles, rank_pad + 8, traces), BF16),
            jax.ShapeDtypeStruct((rows, traces), BF16),
            half,
            half,
        ),
        in_specs=[hbm(), hbm()],
        out_specs=(vmem(),) * 4,
        scratch_shapes=[
            pltpu.VMEM(u.shape, BF16),
            pltpu.VMEM(field.shape, F32),
            pltpu.SemaphoreType.DMA((2,)),
        ],
        compiler_params=pltpu.CompilerParams(vmem_limit_bytes=54400 * 1024),
        cost_estimate=pl.CostEstimate(flops=4 * rows * rows * width, bytes_accessed=1200000, transcendentals=0),
        name="prologue",
    )(u, field)


def product(high, low, c):
    top = c.astype(BF16)
    rest = (c - top.astype(F32)).astype(BF16)
    n = c.shape[1]
    main = jnp.dot(high[...], jnp.concatenate([top, rest], axis=1), preferred_element_type=F32)
    return main[:, :n] + main[:, n:] + jnp.dot(low[...], top, preferred_element_type=F32)


def dot(x, y):
    return jnp.sum(x * y, axis=0, keepdims=True)


def pack(c, out, tails):
    tiles, height, traces = out.shape
    rank_pad = c.shape[0] // tiles
    row = lax.broadcasted_iota(jnp.int32, (height - rank_pad, traces), 0)
    tail = jnp.zeros(row.shape, F32)
    for k, value in enumerate(tails):
        tail = jnp.where(row == k, value, tail)
    tail = tail.astype(BF16)
    c = c.astype(BF16)
    for k in range(tiles):
        out[k, :rank_pad] = c[k * rank_pad : (k + 1) * rank_pad]
        out[k, rank_pad:] = tail


def send(c, known, out, extra):
    norm = dot(known, known)
    factor = jnp.where(norm > 0.0, dot(known, c) / jnp.where(norm > 0.0, norm, 1.0), 0.0)
    factor = jnp.where(jnp.abs(factor) < 1e30, factor, 0.0).astype(BF16).astype(F32)
    rest = c - factor * known
    pack(rest, out, (factor, *extra))
    return rest.astype(BF16).astype(F32) + factor * known


def receive(blocks, known, rank_pad):
    parts = []
    for k in range(blocks.shape[0]):
        factor = blocks[k, rank_pad:].astype(F32)[:1]
        parts.append(blocks[k, :rank_pad].astype(F32) + factor * known[k * rank_pad : (k + 1) * rank_pad])
    return jnp.concatenate(parts, axis=0)


def inverse(scale):
    return jnp.where(scale > 0.0, 1.0 / jnp.where(scale > 0.0, scale, 1.0), 0.0)


def pieces(row):
    first = row.astype(BF16).astype(F32)
    second = (row - first).astype(BF16).astype(F32)
    return first, second, row - first - second


def fill(sums, row):
    sums[...] = jnp.broadcast_to(row, sums.shape)


def first_kernel(rank_pad, ranks, v, blocks, out, high, low, mask_u, mask_v, b0_ref, kept, scales, sums):
    tiles, _, traces = out.shape
    position = lax.axis_index("tile")
    table = ranks[...]
    row = jnp.sum(jnp.where(lax.broadcasted_iota(jnp.int32, table.shape, 0) == position, table, 0), axis=0, keepdims=True)
    col = jnp.sum(jnp.where(lax.broadcasted_iota(jnp.int32, table.shape, 1) == position, table, 0), axis=1, keepdims=True)
    mask_u[...] = mask_of(lambda k: row[:, k : k + 1], tiles, rank_pad, traces)
    mask = mask_of(lambda k: col[k : k + 1], tiles, rank_pad, traces)
    mask_v[...] = mask
    scale = blocks[0, rank_pad:].astype(F32)[:1]
    for k in range(1, tiles):
        scale = jnp.maximum(scale, blocks[k, rank_pad:].astype(F32)[:1])
    fill(scales, scale)
    a0 = jnp.concatenate([blocks[k, :rank_pad].astype(F32) for k in range(tiles)], axis=0)
    a0 = a0 * inverse(scale) * mask
    kept[...] = a0
    gram_store(gram_part(v[...]), high, low)
    b0 = product(high, low, a0) * mask
    fill(sums, dot(a0, b0))
    b0_ref[...] = send(b0, a0, out, [scale])


def second_kernel(rank_pad, high, low, mask, mine, blocks, out, a1_ref, b0_ref, sums):
    scale = blocks[0, rank_pad:].astype(F32)[1:2]
    a0 = mine[...].astype(F32) * inverse(scale) * mask[...]
    b0 = receive(blocks, a0, rank_pad)
    b0_ref[...] = b0
    a1 = product(high, low, b0) * mask[...]
    fill(sums, dot(b0, a1))
    a1_ref[...] = send(a1, a0, out, [])


def third_kernel(rank_pad, high, low, mask, a0, b0, blocks, out, a1_ref, sums):
    a1 = receive(blocks, a0[...], rank_pad)
    a1_ref[...] = a1
    b1 = product(high, low, a1) * mask[...]
    fill(sums, dot(a1, b1))
    send(b1, b0[...], out, [])


def fourth_kernel(rank_pad, high, low, mask, b0, a1, scales, m0, m1, m2, blocks, out, b1_ref):
    b1 = receive(blocks, b0[...], rank_pad)
    b1_ref[...] = b1
    a2 = product(high, low, b1) * mask[...]
    sums = (m0[:1], m1[:1], m2[:1], dot(b1, a2))
    send(a2, a1[...], out, [part for row in sums for part in pieces(row)] + [scales[:1]])


def step(kernel, tiles, rank_pad, spare, kept, name, *args):
    traces = args[-1].shape[-1]
    rows = tiles * rank_pad
    shapes = [jax.ShapeDtypeStruct((tiles, rank_pad + spare, traces), BF16)]
    shapes += [jax.ShapeDtypeStruct(*shape) for shape in kept]
    return pl.pallas_call(
        functools.partial(kernel, rank_pad),
        out_shape=tuple(shapes),
        in_specs=[vmem()] * len(args),
        out_specs=(vmem(),) * len(shapes),
        compiler_params=params(),
        cost_estimate=pl.CostEstimate(flops=6 * rows * rows * traces, bytes_accessed=900000, transcendentals=0),
        name=name,
    )(*args)


def finish_kernel(
    rank_pad, s0, s1, s2, s3, a0, a1, blocks, b0, b1, vt, ut, field, model_hbm, resid_hbm, grad_hbm, bufs, sems
):
    tiles = blocks.shape[0]
    every = [s[...] for s in (s0, s1, s2, s3)]
    scales = [rows[13:14] for rows in every]
    largest = jnp.max(functools.reduce(jnp.maximum, scales), axis=1, keepdims=True)
    shares = [scale * inverse(largest) for scale in scales]
    sums = sum(rows * (share * share) for rows, share in zip(every, shares))
    sums = jnp.sum(sums, axis=1, keepdims=True)
    scale = scales[0] * (1.0 / tiles)
    m0, m1, m2, m3 = (sums[3 * k + 1 : 3 * k + 2] + sums[3 * k + 2 : 3 * k + 3] + sums[3 * k + 3 : 3 * k + 4] for k in range(4))
    alpha = m0 / m1
    gamma = m0 - 2.0 * alpha * m1 + alpha * alpha * m2
    grow = 1.0 + gamma / m0
    delta = grow * grow * m1 - 2.0 * alpha * grow * m2 + alpha * alpha * m3
    alpha_new = gamma / delta
    first = alpha + alpha_new * grow
    second = alpha * alpha_new
    a2 = receive(blocks, a1[...], rank_pad)
    to_model = (scale * (first * a0[...] - second * a1[...])).astype(BF16)
    to_grad = (scale * (a0[...] - first * a1[...] + second * a2)).astype(BF16)
    to_resid = (scale * (first * b0[...] - second * b1[...])).astype(BF16)
    to_both = jnp.concatenate([to_model, to_grad], axis=1)
    step_rows = field.shape[0] // CHUNKS
    copies = []
    for c in range(CHUNKS):
        part = slice(c * step_rows, (c + 1) * step_rows)
        where = pl.ds(c * step_rows, step_rows)
        both = jnp.dot(vt[part], to_both, preferred_element_type=F32)
        bufs[0, part] = both[:, : both.shape[1] // 2]
        bufs[2, part] = both[:, both.shape[1] // 2 :]
        bufs[1, part] = field[part] - jnp.dot(ut[part], to_resid, preferred_element_type=F32)
        for k, out in enumerate((model_hbm, resid_hbm, grad_hbm)):
            copy = pltpu.make_async_copy(bufs.at[k, where], out.at[where], sems.at[k, c])
            copy.start()
            copies.append(copy)
    for copy in copies:
        copy.wait()


def finish(sums, a0, a1, blocks, b0, b1, vt, ut, field, rank_pad):
    out = jax.ShapeDtypeStruct(field.shape, F32)
    return pl.pallas_call(
        functools.partial(finish_kernel, rank_pad),
        out_shape=(out, out, out),
        in_specs=[vmem()] * 12,
        out_specs=(hbm(), hbm(), hbm()),
        scratch_shapes=[pltpu.VMEM((3, *field.shape), F32), pltpu.SemaphoreType.DMA((3, CHUNKS))],
        compiler_params=params(),
        cost_estimate=pl.CostEstimate(flops=250000000, bytes_accessed=3000000, transcendentals=0),
        name="finish",
    )(*sums, a0, a1, blocks, b0, b1, vt, ut, field)


def by_kernels(u_tiles, v_tiles, tile_ranks, recorded):
    _, _, tiles, rank_pad, width = u_tiles.shape
    traces = recorded.shape[2]
    freqs = lax.axis_size("freq")
    rows = tiles * rank_pad
    u = u_tiles.reshape(rows, width)
    v = v_tiles.reshape(rows, width)
    field = recorded[0]

    def swap(blocks):
        return lax.all_to_all(blocks, "tile", split_axis=0, concat_axis=0, tiled=True)

    out, mine, high_u, low_u = prologue(u, field, tiles, rank_pad)
    out, v = lax.optimization_barrier((out, v))
    wide, short, half = ((rows, traces), F32), ((8, traces), F32), ((rows, rows), BF16)
    kept = (half, half, wide, wide, wide, wide, short, short)
    out, high_v, low_v, mask_u, mask_v, b0_col, a0, scales, m0 = step(
        first_kernel, tiles, rank_pad, 8, kept, "first", tile_ranks[0], v, swap(out)
    )
    out, a1_row, b0, m1 = step(
        second_kernel, tiles, rank_pad, 8, (wide, wide, short), "second", high_u, low_u, mask_u, mine, swap(out)
    )
    out, a1, m2 = step(
        third_kernel, tiles, rank_pad, 8, (wide, short), "third", high_v, low_v, mask_v, a0, b0_col, swap(out)
    )
    known = (high_u, low_u, mask_u, b0, a1_row, scales, m0, m1, m2)
    out, b1 = step(fourth_kernel, tiles, rank_pad, 16, (wide,), "fourth", *known, swap(out))
    blocks = swap(out)
    sums, u, v = lax.optimization_barrier((jnp.sum(blocks[:, rank_pad:].astype(F32), axis=0), u, v))
    whole = [sums]
    for shift in range(1, 4):
        whole.append(lax.ppermute(sums, "freq", [(k, k ^ shift) for k in range(freqs)]))
    model, residual, gradient = finish(whole, a0, a1, blocks, b0, b1, v.T, u.T, field, rank_pad)
    return model[None], residual[None], gradient[None]


def by_arrays(u_tiles, v_tiles, tile_ranks, recorded):
    _, tile_dev, tiles, rank_pad, width = u_tiles.shape
    traces = recorded.shape[2]
    freqs = lax.axis_size("freq")
    position = lax.axis_index("tile")
    levels = jnp.arange(rank_pad, dtype=jnp.int32)
    rank_rows = lax.dynamic_slice_in_dim(tile_ranks[0], position * tile_dev, tile_dev, 0)
    rank_cols = lax.dynamic_slice_in_dim(tile_ranks[0], position * tile_dev, tile_dev, 1)
    mask_rows = (levels < rank_rows[..., None]).astype(F32)
    mask_cols = (levels < rank_cols.T[..., None]).astype(F32)
    u = u_tiles[0].reshape(tile_dev, tiles * rank_pad, width)
    v = jnp.swapaxes(v_tiles[0], 0, 1).reshape(tile_dev, tiles * rank_pad, width)
    mask_u = mask_rows.reshape(tile_dev, tiles * rank_pad, 1)
    mask_v = mask_cols.reshape(tile_dev, tiles * rank_pad, 1)

    def gram_of(x):
        return jnp.einsum("drb,dsb->drs", x, x, preferred_element_type=F32)

    def swap(c):
        c = c.reshape(tile_dev, tiles, rank_pad, traces)
        c = lax.all_to_all(c, "tile", split_axis=1, concat_axis=0, tiled=True)
        return jnp.swapaxes(c, 0, 1).reshape(tile_dev, tiles * rank_pad, traces)

    def times(g, c, mask):
        return mask * jnp.einsum("drs,dst->drt", g, c, precision=HIGH)

    field = recorded.reshape(tile_dev, width, traces)
    gram_u, gram_v = gram_of(u), gram_of(v)
    a0 = mask_u * jnp.einsum("drb,dbt->drt", u, field.astype(BF16), preferred_element_type=F32)
    largest = lax.pmax(lax.pmax(jnp.max(jnp.abs(a0)), "tile"), "freq")
    scale = jnp.where(largest > 0.0, largest, 1.0)
    a0 = swap(a0 * (2.0**-20 / scale))
    b0v = times(gram_v, a0, mask_v)
    b0 = swap(b0v)
    a1u = times(gram_u, b0, mask_u)
    a1 = swap(a1u)
    b1v = times(gram_v, a1, mask_v)
    b1 = swap(b1v)
    a2u = times(gram_u, b1, mask_u)
    a2 = swap(a2u)
    parts = jnp.stack([jnp.sum(x * y) for x, y in ((a0, b0v), (b0, a1u), (a1, b1v), (b1, a2u))])
    m0, m1, m2, m3 = lax.psum(lax.psum(parts, "tile"), "freq")
    alpha = m0 / m1
    gamma = m0 - 2.0 * alpha * m1 + alpha * alpha * m2
    grow = 1.0 + gamma / m0
    delta = grow * grow * m1 - 2.0 * alpha * grow * m2 + alpha * alpha * m3
    alpha_new = gamma / delta
    first = alpha + alpha_new * grow
    second = alpha * alpha_new

    def expand(x, c):
        image = jnp.einsum("drb,drt->dbt", x.astype(F32), c, precision=HIGH)
        return image.reshape(1, tile_dev * width, traces)

    back = scale * 2.0**20
    model = back * expand(v, first * a0 - second * a1)
    gradient = back * expand(v, a0 - first * a1 + second * a2)
    residual = recorded - back * expand(u, first * b0 - second * b1)
    return model, residual, gradient


def local(u_tiles, v_tiles, tile_ranks, recorded):
    _, tile_dev, tiles, rank_pad, _ = u_tiles.shape
    small = tile_dev == 1 and tiles * rank_pad <= KERNEL_ROWS and lax.axis_size("freq") == 4
    return (by_kernels if small else by_arrays)(u_tiles, v_tiles, tile_ranks, recorded)


def solution(mesh):
    placed = (
        P("freq", "tile", None, None, None),
        P("freq", None, "tile", None, None),
        P("freq", None, None),
        P("freq", "tile", None),
    )
    out = P("freq", "tile", None)
    return jax.shard_map(local, mesh=mesh, in_specs=placed, out_specs=(out, out, out), check_vma=False)
```

```python
import functools

import jax
import jax.numpy as jnp
from jax import lax
from jax.experimental import pallas as pl
from jax.experimental.pallas import tpu as pltpu
from jax.sharding import PartitionSpec as P

HIGH = lax.Precision.HIGHEST
F32 = jnp.float32
BF16 = jnp.bfloat16
KERNEL_ROWS = 640
CHUNKS = 4
BLOCK = 256
TAIL = 8


def vmem():
    return pl.BlockSpec(memory_space=pltpu.VMEM)


def hbm():
    return pl.BlockSpec(memory_space=pltpu.HBM)


def params():
    return pltpu.CompilerParams(vmem_limit_bytes=12 * 1024 * 1024)


def gram_columns(rows):
    return [(c, min(BLOCK, rows - c)) for c in range(0, rows, BLOCK)]


def gram_part(x):
    return [
        lax.dot_general(x[c:], x[c : c + n], (((1,), (1,)), ((), ())), preferred_element_type=F32)
        for c, n in gram_columns(x.shape[0])
    ]


def gram_store(parts, high, low):
    for (c, n), g in zip(gram_columns(high.shape[0]), parts):
        top = g.astype(BF16)
        rest = (g - top.astype(F32)).astype(BF16)
        high[c:, c : c + n] = top
        low[c:, c : c + n] = rest
        if g.shape[0] > n:
            above = g[n:].T
            top = above.astype(BF16)
            high[c : c + n, c + n :] = top
            low[c : c + n, c + n :] = (above - top.astype(F32)).astype(BF16)


def mask_of(rank, tiles, rank_pad, traces):
    level = lax.broadcasted_iota(jnp.int32, (rank_pad, traces), 0)
    return jnp.concatenate([jnp.where(level < rank(k), 1.0, 0.0) for k in range(tiles)], axis=0)


def prologue_kernel(u_hbm, field_hbm, out, kept, high, low, u, field, sems):
    copies = [pltpu.make_async_copy(u_hbm, u, sems.at[0]), pltpu.make_async_copy(field_hbm, field, sems.at[1])]
    for copy in copies:
        copy.start()
    for copy in copies:
        copy.wait()
    mine = jnp.dot(u[...], field[...].astype(BF16), preferred_element_type=F32)
    kept[...] = mine.astype(BF16)
    pack(mine, out, [jnp.max(jnp.abs(mine), axis=0, keepdims=True)])
    gram_store(gram_part(u[...]), high, low)


def prologue(u, field, tiles, rank_pad):
    rows, width = u.shape
    traces = field.shape[1]
    half = jax.ShapeDtypeStruct((rows, rows), BF16)
    return pl.pallas_call(
        prologue_kernel,
        out_shape=(
            jax.ShapeDtypeStruct((tiles, rank_pad + TAIL, traces), BF16),
            jax.ShapeDtypeStruct((rows, traces), BF16),
            half,
            half,
        ),
        in_specs=[hbm(), hbm()],
        out_specs=(vmem(),) * 4,
        scratch_shapes=[
            pltpu.VMEM(u.shape, BF16),
            pltpu.VMEM(field.shape, F32),
            pltpu.SemaphoreType.DMA((2,)),
        ],
        compiler_params=pltpu.CompilerParams(vmem_limit_bytes=54400 * 1024),
        cost_estimate=pl.CostEstimate(flops=4 * rows * rows * width, bytes_accessed=1200000, transcendentals=0),
        name="prologue",
    )(u, field)


def product(high, low, c):
    top = c.astype(BF16)
    rest = (c - top.astype(F32)).astype(BF16)
    n = c.shape[1]
    main = jnp.dot(high[...], jnp.concatenate([top, rest], axis=1), preferred_element_type=F32)
    return main[:, :n] + main[:, n:] + jnp.dot(low[...], top, preferred_element_type=F32)


def dot(x, y):
    return jnp.sum(x * y, axis=0, keepdims=True)


def pack(c, out, tails):
    tiles, height, traces = out.shape
    rank_pad = c.shape[0] // tiles
    row = lax.broadcasted_iota(jnp.int32, (height - rank_pad, traces), 0)
    tail = jnp.zeros(row.shape, F32)
    for k, value in enumerate(tails):
        tail = jnp.where(row == k, value, tail)
    tail = tail.astype(BF16)
    c = c.astype(BF16)
    for k in range(tiles):
        out[k, :rank_pad] = c[k * rank_pad : (k + 1) * rank_pad]
        out[k, rank_pad:] = tail


def send(c, known, out, extra):
    norm = dot(known, known)
    factor = jnp.where(norm > 0.0, dot(known, c) / jnp.where(norm > 0.0, norm, 1.0), 0.0)
    factor = jnp.where(jnp.abs(factor) < 1e30, factor, 0.0).astype(BF16).astype(F32)
    rest = c - factor * known
    pack(rest, out, (factor, *extra))
    return rest.astype(BF16).astype(F32) + factor * known


def receive(blocks, known, rank_pad):
    parts = []
    for k in range(blocks.shape[0]):
        factor = blocks[k, rank_pad:].astype(F32)[:1]
        parts.append(blocks[k, :rank_pad].astype(F32) + factor * known[k * rank_pad : (k + 1) * rank_pad])
    return jnp.concatenate(parts, axis=0)


def inverse(scale):
    return jnp.where(scale > 0.0, 1.0 / jnp.where(scale > 0.0, scale, 1.0), 0.0)


def pieces(row):
    first = row.astype(BF16).astype(F32)
    second = (row - first).astype(BF16).astype(F32)
    return first, second, row - first - second


def gathered(blocks, rank_pad):
    total = blocks[0, rank_pad:].astype(F32)
    for k in range(1, blocks.shape[0]):
        total += blocks[k, rank_pad:].astype(F32)
    return total[1:2] + total[2:3] + total[3:4]


def fill(sums, row):
    sums[...] = jnp.broadcast_to(row, sums.shape)


def first_kernel(rank_pad, ranks, v, blocks, out, high, low, mask_u, mask_v, b0_ref, kept, scales):
    tiles, _, traces = out.shape
    position = lax.axis_index("tile")
    table = ranks[...]
    row = jnp.sum(jnp.where(lax.broadcasted_iota(jnp.int32, table.shape, 0) == position, table, 0), axis=0, keepdims=True)
    col = jnp.sum(jnp.where(lax.broadcasted_iota(jnp.int32, table.shape, 1) == position, table, 0), axis=1, keepdims=True)
    mask_u[...] = mask_of(lambda k: row[:, k : k + 1], tiles, rank_pad, traces)
    mask = mask_of(lambda k: col[k : k + 1], tiles, rank_pad, traces)
    mask_v[...] = mask
    scale = blocks[0, rank_pad:].astype(F32)[:1]
    for k in range(1, tiles):
        scale = jnp.maximum(scale, blocks[k, rank_pad:].astype(F32)[:1])
    fill(scales, scale)
    a0 = jnp.concatenate([blocks[k, :rank_pad].astype(F32) for k in range(tiles)], axis=0)
    a0 = a0 * inverse(scale) * mask
    kept[...] = a0
    gram_store(gram_part(v[...]), high, low)
    b0 = product(high, low, a0) * mask
    b0_ref[...] = send(b0, a0, out, [*pieces(dot(a0, b0)), scale])


def second_kernel(rank_pad, high, low, mask, mine, blocks, out, a1_ref, b0_ref, sums):
    fill(sums, gathered(blocks, rank_pad))
    scale = blocks[0, rank_pad:].astype(F32)[4:5]
    a0 = mine[...].astype(F32) * inverse(scale) * mask[...]
    b0 = receive(blocks, a0, rank_pad)
    b0_ref[...] = b0
    a1 = product(high, low, b0) * mask[...]
    a1_ref[...] = send(a1, a0, out, pieces(dot(b0, a1)))


def third_kernel(rank_pad, high, low, mask, a0, b0, blocks, out, a1_ref, sums):
    fill(sums, gathered(blocks, rank_pad))
    a1 = receive(blocks, a0[...], rank_pad)
    a1_ref[...] = a1
    b1 = product(high, low, a1) * mask[...]
    send(b1, b0[...], out, pieces(dot(a1, b1)))


def fourth_kernel(rank_pad, high, low, mask, b0, a1, scales, m0, m1, blocks, out, b1_ref, sums):
    row = lax.broadcasted_iota(jnp.int32, sums.shape, 0)
    known = jnp.where(row == 4, m0[...], jnp.where(row == 5, m1[...], 0.0))
    sums[...] = jnp.where(row == 6, gathered(blocks, rank_pad), jnp.where(row == 7, scales[...], known))
    b1 = receive(blocks, b0[...], rank_pad)
    b1_ref[...] = b1
    a2 = product(high, low, b1) * mask[...]
    send(a2, a1[...], out, pieces(dot(b1, a2)))


def step(kernel, tiles, rank_pad, kept, name, *args):
    traces = args[-1].shape[-1]
    rows = tiles * rank_pad
    shapes = [jax.ShapeDtypeStruct((tiles, rank_pad + TAIL, traces), BF16)]
    shapes += [jax.ShapeDtypeStruct(*shape) for shape in kept]
    return pl.pallas_call(
        functools.partial(kernel, rank_pad),
        out_shape=tuple(shapes),
        in_specs=[vmem()] * len(args),
        out_specs=(vmem(),) * len(shapes),
        compiler_params=params(),
        cost_estimate=pl.CostEstimate(flops=6 * rows * rows * traces, bytes_accessed=900000, transcendentals=0),
        name=name,
    )(*args)


def finish_kernel(
    rank_pad, s0, s1, s2, s3, a0, a1, blocks, b0, b1, vt, ut, field, model_hbm, resid_hbm, grad_hbm, bufs, sems
):
    every = [s[...] for s in (s0, s1, s2, s3)]
    scales = [rows[7:8] for rows in every]
    largest = jnp.max(functools.reduce(jnp.maximum, scales), axis=1, keepdims=True)
    shares = [scale * inverse(largest) for scale in scales]
    sums = sum(rows * (share * share) for rows, share in zip(every, shares))
    sums = jnp.sum(sums, axis=1, keepdims=True)
    scale = scales[0]
    m0, m1, m2 = sums[4:5], sums[5:6], sums[6:7]
    m3 = sums[1:2] + sums[2:3] + sums[3:4]
    alpha = m0 / m1
    gamma = m0 - 2.0 * alpha * m1 + alpha * alpha * m2
    grow = 1.0 + gamma / m0
    delta = grow * grow * m1 - 2.0 * alpha * grow * m2 + alpha * alpha * m3
    alpha_new = gamma / delta
    first = alpha + alpha_new * grow
    second = alpha * alpha_new
    a2 = receive(blocks, a1[...], rank_pad)
    to_model = (scale * (first * a0[...] - second * a1[...])).astype(BF16)
    to_grad = (scale * (a0[...] - first * a1[...] + second * a2)).astype(BF16)
    to_resid = (scale * (first * b0[...] - second * b1[...])).astype(BF16)
    to_both = jnp.concatenate([to_model, to_grad], axis=1)
    step_rows = field.shape[0] // CHUNKS
    copies = []
    for c in range(CHUNKS):
        part = slice(c * step_rows, (c + 1) * step_rows)
        where = pl.ds(c * step_rows, step_rows)
        both = jnp.dot(vt[part], to_both, preferred_element_type=F32)
        bufs[0, part] = both[:, : both.shape[1] // 2]
        bufs[2, part] = both[:, both.shape[1] // 2 :]
        bufs[1, part] = field[part] - jnp.dot(ut[part], to_resid, preferred_element_type=F32)
        for k, out in enumerate((model_hbm, resid_hbm, grad_hbm)):
            copy = pltpu.make_async_copy(bufs.at[k, where], out.at[where], sems.at[k, c])
            copy.start()
            copies.append(copy)
    for copy in copies:
        copy.wait()


def finish(sums, a0, a1, blocks, b0, b1, vt, ut, field, rank_pad):
    out = jax.ShapeDtypeStruct(field.shape, F32)
    return pl.pallas_call(
        functools.partial(finish_kernel, rank_pad),
        out_shape=(out, out, out),
        in_specs=[vmem()] * 12,
        out_specs=(hbm(), hbm(), hbm()),
        scratch_shapes=[pltpu.VMEM((3, *field.shape), F32), pltpu.SemaphoreType.DMA((3, CHUNKS))],
        compiler_params=params(),
        cost_estimate=pl.CostEstimate(flops=250000000, bytes_accessed=3000000, transcendentals=0),
        name="finish",
    )(*sums, a0, a1, blocks, b0, b1, vt, ut, field)


def by_kernels(u_tiles, v_tiles, tile_ranks, recorded):
    _, _, tiles, rank_pad, width = u_tiles.shape
    traces = recorded.shape[2]
    freqs = lax.axis_size("freq")
    rows = tiles * rank_pad
    u = u_tiles.reshape(rows, width)
    v = v_tiles.reshape(rows, width)
    field = recorded[0]

    def swap(blocks):
        return lax.all_to_all(blocks, "tile", split_axis=0, concat_axis=0, tiled=True)

    out, mine, high_u, low_u = prologue(u, field, tiles, rank_pad)
    out, v = lax.optimization_barrier((out, v))
    wide, short, half = ((rows, traces), F32), ((8, traces), F32), ((rows, rows), BF16)
    kept = (half, half, wide, wide, wide, wide, short)
    out, high_v, low_v, mask_u, mask_v, b0_col, a0, scales = step(
        first_kernel, tiles, rank_pad, kept, "first", tile_ranks[0], v, swap(out)
    )
    out, a1_row, b0, m0 = step(
        second_kernel, tiles, rank_pad, (wide, wide, short), "second", high_u, low_u, mask_u, mine, swap(out)
    )
    out, a1, m1 = step(
        third_kernel, tiles, rank_pad, (wide, short), "third", high_v, low_v, mask_v, a0, b0_col, swap(out)
    )
    known = (high_u, low_u, mask_u, b0, a1_row, scales, m0, m1)
    out, b1, sums = step(fourth_kernel, tiles, rank_pad, (wide, short), "fourth", *known, swap(out))
    blocks = swap(out)
    sums = sums + jnp.sum(blocks[:, rank_pad:].astype(F32), axis=0)
    sums, u, v = lax.optimization_barrier((sums, u, v))
    whole = [sums]
    for shift in range(1, 4):
        whole.append(lax.ppermute(sums, "freq", [(k, k ^ shift) for k in range(freqs)]))
    model, residual, gradient = finish(whole, a0, a1, blocks, b0, b1, v.T, u.T, field, rank_pad)
    return model[None], residual[None], gradient[None]


def by_arrays(u_tiles, v_tiles, tile_ranks, recorded):
    _, tile_dev, tiles, rank_pad, width = u_tiles.shape
    traces = recorded.shape[2]
    freqs = lax.axis_size("freq")
    position = lax.axis_index("tile")
    levels = jnp.arange(rank_pad, dtype=jnp.int32)
    rank_rows = lax.dynamic_slice_in_dim(tile_ranks[0], position * tile_dev, tile_dev, 0)
    rank_cols = lax.dynamic_slice_in_dim(tile_ranks[0], position * tile_dev, tile_dev, 1)
    mask_rows = (levels < rank_rows[..., None]).astype(F32)
    mask_cols = (levels < rank_cols.T[..., None]).astype(F32)
    u = u_tiles[0].reshape(tile_dev, tiles * rank_pad, width)
    v = jnp.swapaxes(v_tiles[0], 0, 1).reshape(tile_dev, tiles * rank_pad, width)
    mask_u = mask_rows.reshape(tile_dev, tiles * rank_pad, 1)
    mask_v = mask_cols.reshape(tile_dev, tiles * rank_pad, 1)

    def gram_of(x):
        return jnp.einsum("drb,dsb->drs", x, x, preferred_element_type=F32)

    def swap(c):
        c = c.reshape(tile_dev, tiles, rank_pad, traces)
        c = lax.all_to_all(c, "tile", split_axis=1, concat_axis=0, tiled=True)
        return jnp.swapaxes(c, 0, 1).reshape(tile_dev, tiles * rank_pad, traces)

    def times(g, c, mask):
        return mask * jnp.einsum("drs,dst->drt", g, c, precision=HIGH)

    field = recorded.reshape(tile_dev, width, traces)
    gram_u, gram_v = gram_of(u), gram_of(v)
    a0 = mask_u * jnp.einsum("drb,dbt->drt", u, field.astype(BF16), preferred_element_type=F32)
    largest = lax.pmax(lax.pmax(jnp.max(jnp.abs(a0)), "tile"), "freq")
    scale = jnp.where(largest > 0.0, largest, 1.0)
    a0 = swap(a0 * (2.0**-20 / scale))
    b0v = times(gram_v, a0, mask_v)
    b0 = swap(b0v)
    a1u = times(gram_u, b0, mask_u)
    a1 = swap(a1u)
    b1v = times(gram_v, a1, mask_v)
    b1 = swap(b1v)
    a2u = times(gram_u, b1, mask_u)
    a2 = swap(a2u)
    parts = jnp.stack([jnp.sum(x * y) for x, y in ((a0, b0v), (b0, a1u), (a1, b1v), (b1, a2u))])
    m0, m1, m2, m3 = lax.psum(lax.psum(parts, "tile"), "freq")
    alpha = m0 / m1
    gamma = m0 - 2.0 * alpha * m1 + alpha * alpha * m2
    grow = 1.0 + gamma / m0
    delta = grow * grow * m1 - 2.0 * alpha * grow * m2 + alpha * alpha * m3
    alpha_new = gamma / delta
    first = alpha + alpha_new * grow
    second = alpha * alpha_new

    def expand(x, c):
        image = jnp.einsum("drb,drt->dbt", x.astype(F32), c, precision=HIGH)
        return image.reshape(1, tile_dev * width, traces)

    back = scale * 2.0**20
    model = back * expand(v, first * a0 - second * a1)
    gradient = back * expand(v, a0 - first * a1 + second * a2)
    residual = recorded - back * expand(u, first * b0 - second * b1)
    return model, residual, gradient


def local(u_tiles, v_tiles, tile_ranks, recorded):
    _, tile_dev, tiles, rank_pad, _ = u_tiles.shape
    small = tile_dev == 1 and tiles * rank_pad <= KERNEL_ROWS and lax.axis_size("freq") == 4
    return (by_kernels if small else by_arrays)(u_tiles, v_tiles, tile_ranks, recorded)


def solution(mesh):
    placed = (
        P("freq", "tile", None, None, None),
        P("freq", None, "tile", None, None),
        P("freq", None, None),
        P("freq", "tile", None),
    )
    out = P("freq", "tile", None)
    return jax.shard_map(local, mesh=mesh, in_specs=placed, out_specs=(out, out, out), check_vma=False)
```

```python
import functools

import jax
import jax.numpy as jnp
from jax import lax
from jax.experimental import pallas as pl
from jax.experimental.pallas import tpu as pltpu
from jax.sharding import PartitionSpec as P

HIGH = lax.Precision.HIGHEST
F32 = jnp.float32
BF16 = jnp.bfloat16
KERNEL_ROWS = 640
CHUNKS = 4
BLOCK = 256
TAIL = 8


def vmem():
    return pl.BlockSpec(memory_space=pltpu.VMEM)


def hbm():
    return pl.BlockSpec(memory_space=pltpu.HBM)


def params():
    return pltpu.CompilerParams(vmem_limit_bytes=12 * 1024 * 1024)


def gram_columns(rows):
    return [(c, min(BLOCK, rows - c)) for c in range(0, rows, BLOCK)]


def gram_part(x):
    return [
        lax.dot_general(x[c:], x[c : c + n], (((1,), (1,)), ((), ())), preferred_element_type=F32)
        for c, n in gram_columns(x.shape[0])
    ]


def gram_store(parts, high, low):
    for (c, n), g in zip(gram_columns(high.shape[0]), parts):
        top = g.astype(BF16)
        rest = (g - top.astype(F32)).astype(BF16)
        high[c:, c : c + n] = top
        low[c:, c : c + n] = rest
        if g.shape[0] > n:
            above = g[n:].T
            top = above.astype(BF16)
            high[c : c + n, c + n :] = top
            low[c : c + n, c + n :] = (above - top.astype(F32)).astype(BF16)


def mask_of(rank, tiles, rank_pad, traces):
    level = lax.broadcasted_iota(jnp.int32, (rank_pad, traces), 0)
    return jnp.concatenate([jnp.where(level < rank(k), 1.0, 0.0) for k in range(tiles)], axis=0)


def prologue_kernel(u_hbm, field_hbm, out, kept, high, low, u, field, sems):
    copies = [pltpu.make_async_copy(u_hbm, u, sems.at[0]), pltpu.make_async_copy(field_hbm, field, sems.at[1])]
    for copy in copies:
        copy.start()
    for copy in copies:
        copy.wait()
    mine = jnp.dot(u[...], field[...].astype(BF16), preferred_element_type=F32)
    kept[...] = mine.astype(BF16)
    pack(mine, out, [jnp.max(jnp.abs(mine), axis=0, keepdims=True)])
    gram_store(gram_part(u[...]), high, low)


def prologue(u, field, tiles, rank_pad):
    rows, width = u.shape
    traces = field.shape[1]
    half = jax.ShapeDtypeStruct((rows, rows), BF16)
    return pl.pallas_call(
        prologue_kernel,
        out_shape=(
            jax.ShapeDtypeStruct((tiles, rank_pad + TAIL, traces), BF16),
            jax.ShapeDtypeStruct((rows, traces), BF16),
            half,
            half,
        ),
        in_specs=[hbm(), hbm()],
        out_specs=(vmem(),) * 4,
        scratch_shapes=[
            pltpu.VMEM(u.shape, BF16),
            pltpu.VMEM(field.shape, F32),
            pltpu.SemaphoreType.DMA((2,)),
        ],
        compiler_params=pltpu.CompilerParams(vmem_limit_bytes=54400 * 1024),
        cost_estimate=pl.CostEstimate(flops=4 * rows * rows * width, bytes_accessed=1200000, transcendentals=0),
        name="prologue",
    )(u, field)


def product(high, low, c):
    top = c.astype(BF16)
    rest = (c - top.astype(F32)).astype(BF16)
    n = c.shape[1]
    main = jnp.dot(high[...], jnp.concatenate([top, rest], axis=1), preferred_element_type=F32)
    return main[:, :n] + main[:, n:] + jnp.dot(low[...], top, preferred_element_type=F32)


def dot(x, y):
    return jnp.sum(x * y, axis=0, keepdims=True)


def pack(c, out, tails):
    tiles, height, traces = out.shape
    rank_pad = c.shape[0] // tiles
    row = lax.broadcasted_iota(jnp.int32, (height - rank_pad, traces), 0)
    tail = jnp.zeros(row.shape, F32)
    for k, value in enumerate(tails):
        tail = jnp.where(row == k, value, tail)
    tail = tail.astype(BF16)
    c = c.astype(BF16)
    for k in range(tiles):
        out[k, :rank_pad] = c[k * rank_pad : (k + 1) * rank_pad]
        out[k, rank_pad:] = tail


def send(c, known, out, extra):
    norm = dot(known, known)
    factor = jnp.where(norm > 0.0, dot(known, c) / jnp.where(norm > 0.0, norm, 1.0), 0.0)
    factor = jnp.where(jnp.abs(factor) < 1e30, factor, 0.0).astype(BF16).astype(F32)
    rest = c - factor * known
    pack(rest, out, (factor, *extra))
    return rest.astype(BF16).astype(F32) + factor * known


def receive(blocks, known, rank_pad):
    parts = []
    for k in range(blocks.shape[0]):
        factor = blocks[k, rank_pad:].astype(F32)[:1]
        parts.append(blocks[k, :rank_pad].astype(F32) + factor * known[k * rank_pad : (k + 1) * rank_pad])
    return jnp.concatenate(parts, axis=0)


def inverse(scale):
    return jnp.where(scale > 0.0, 1.0 / jnp.where(scale > 0.0, scale, 1.0), 0.0)


def pieces(row):
    first = row.astype(BF16).astype(F32)
    second = (row - first).astype(BF16).astype(F32)
    return first, second, row - first - second


def gathered(blocks, rank_pad):
    total = blocks[0, rank_pad:].astype(F32)
    for k in range(1, blocks.shape[0]):
        total += blocks[k, rank_pad:].astype(F32)
    return total[1:2] + total[2:3] + total[3:4]


def fill(sums, row):
    sums[...] = jnp.broadcast_to(row, sums.shape)


def first_kernel(rank_pad, ranks, v, blocks, out, high, low, mask_u, mask_v, b0_ref, kept, scales):
    tiles, _, traces = out.shape
    position = lax.axis_index("tile")
    table = ranks[...]
    row = jnp.sum(jnp.where(lax.broadcasted_iota(jnp.int32, table.shape, 0) == position, table, 0), axis=0, keepdims=True)
    col = jnp.sum(jnp.where(lax.broadcasted_iota(jnp.int32, table.shape, 1) == position, table, 0), axis=1, keepdims=True)
    mask_u[...] = mask_of(lambda k: row[:, k : k + 1], tiles, rank_pad, traces)
    mask = mask_of(lambda k: col[k : k + 1], tiles, rank_pad, traces)
    mask_v[...] = mask
    scale = blocks[0, rank_pad:].astype(F32)[:1]
    for k in range(1, tiles):
        scale = jnp.maximum(scale, blocks[k, rank_pad:].astype(F32)[:1])
    fill(scales, scale)
    a0 = jnp.concatenate([blocks[k, :rank_pad].astype(F32) for k in range(tiles)], axis=0)
    a0 = a0 * inverse(scale) * mask
    kept[...] = a0
    gram_store(gram_part(v[...]), high, low)
    b0 = product(high, low, a0) * mask
    b0_ref[...] = send(b0, a0, out, [*pieces(dot(a0, b0)), scale])


def second_kernel(rank_pad, high, low, mask, mine, blocks, out, a1_ref, b0_ref, sums):
    fill(sums, gathered(blocks, rank_pad))
    scale = blocks[0, rank_pad:].astype(F32)[4:5]
    a0 = mine[...].astype(F32) * inverse(scale) * mask[...]
    b0 = receive(blocks, a0, rank_pad)
    b0_ref[...] = b0
    a1 = product(high, low, b0) * mask[...]
    a1_ref[...] = send(a1, a0, out, pieces(dot(b0, a1)))


def third_kernel(rank_pad, high, low, mask, a0, b0, blocks, out, a1_ref, sums):
    fill(sums, gathered(blocks, rank_pad))
    a1 = receive(blocks, a0[...], rank_pad)
    a1_ref[...] = a1
    b1 = product(high, low, a1) * mask[...]
    send(b1, b0[...], out, pieces(dot(a1, b1)))


def fourth_kernel(rank_pad, high, low, mask, b0, a1, scales, m0, m1, blocks, out, b1_ref, sums):
    row = lax.broadcasted_iota(jnp.int32, sums.shape, 0)
    known = jnp.where(row == 4, m0[...], jnp.where(row == 5, m1[...], 0.0))
    sums[...] = jnp.where(row == 6, gathered(blocks, rank_pad), jnp.where(row == 7, scales[...], known))
    b1 = receive(blocks, b0[...], rank_pad)
    b1_ref[...] = b1
    a2 = product(high, low, b1) * mask[...]
    send(a2, a1[...], out, pieces(dot(b1, a2)))


def step(kernel, tiles, rank_pad, kept, name, *args):
    traces = args[-1].shape[-1]
    rows = tiles * rank_pad
    shapes = [jax.ShapeDtypeStruct((tiles, rank_pad + TAIL, traces), BF16)]
    shapes += [jax.ShapeDtypeStruct(*shape) for shape in kept]
    return pl.pallas_call(
        functools.partial(kernel, rank_pad),
        out_shape=tuple(shapes),
        in_specs=[vmem()] * len(args),
        out_specs=(vmem(),) * len(shapes),
        compiler_params=params(),
        cost_estimate=pl.CostEstimate(flops=6 * rows * rows * traces, bytes_accessed=900000, transcendentals=0),
        name=name,
    )(*args)


def finish_kernel(
    rank_pad, s0, s1, s2, s3, a0, a1, blocks, b0, b1, vt, ut, field, model_hbm, resid_hbm, grad_hbm, bufs, sems
):
    every = [s[...] for s in (s0, s1, s2, s3)]
    scales = [rows[7:8] for rows in every]
    largest = jnp.max(functools.reduce(jnp.maximum, scales), axis=1, keepdims=True)
    shares = [scale * inverse(largest) for scale in scales]
    sums = sum(rows * (share * share) for rows, share in zip(every, shares))
    sums = jnp.sum(sums, axis=1, keepdims=True)
    scale = scales[0]
    m0, m1, m2 = sums[4:5], sums[5:6], sums[6:7]
    m3 = sums[1:2] + sums[2:3] + sums[3:4]
    alpha = m0 / m1
    gamma = m0 - 2.0 * alpha * m1 + alpha * alpha * m2
    grow = 1.0 + gamma / m0
    delta = grow * grow * m1 - 2.0 * alpha * grow * m2 + alpha * alpha * m3
    alpha_new = gamma / delta
    first = alpha + alpha_new * grow
    second = alpha * alpha_new
    a2 = receive(blocks, a1[...], rank_pad)
    to_model = (scale * (first * a0[...] - second * a1[...])).astype(BF16)
    to_grad = (scale * (a0[...] - first * a1[...] + second * a2)).astype(BF16)
    to_resid = (scale * (first * b0[...] - second * b1[...])).astype(BF16)
    to_both = jnp.concatenate([to_model, to_grad], axis=1)
    step_rows = field.shape[0] // CHUNKS
    copies = []
    for c in range(CHUNKS):
        part = slice(c * step_rows, (c + 1) * step_rows)
        where = pl.ds(c * step_rows, step_rows)
        bufs[1, part] = field[part] - jnp.dot(ut[part], to_resid, preferred_element_type=F32)
        copies.append(pltpu.make_async_copy(bufs.at[1, where], resid_hbm.at[where], sems.at[1, c]))
        copies[-1].start()
        both = jnp.dot(vt[part], to_both, preferred_element_type=F32)
        bufs[0, part] = both[:, : both.shape[1] // 2]
        bufs[2, part] = both[:, both.shape[1] // 2 :]
        for k, out in ((0, model_hbm), (2, grad_hbm)):
            copies.append(pltpu.make_async_copy(bufs.at[k, where], out.at[where], sems.at[k, c]))
            copies[-1].start()
    for copy in copies:
        copy.wait()


def finish(sums, a0, a1, blocks, b0, b1, vt, ut, field, rank_pad):
    out = jax.ShapeDtypeStruct(field.shape, F32)
    return pl.pallas_call(
        functools.partial(finish_kernel, rank_pad),
        out_shape=(out, out, out),
        in_specs=[vmem()] * 12,
        out_specs=(hbm(), hbm(), hbm()),
        scratch_shapes=[pltpu.VMEM((3, *field.shape), F32), pltpu.SemaphoreType.DMA((3, CHUNKS))],
        compiler_params=params(),
        cost_estimate=pl.CostEstimate(flops=250000000, bytes_accessed=3000000, transcendentals=0),
        name="finish",
    )(*sums, a0, a1, blocks, b0, b1, vt, ut, field)


def by_kernels(u_tiles, v_tiles, tile_ranks, recorded):
    _, _, tiles, rank_pad, width = u_tiles.shape
    traces = recorded.shape[2]
    freqs = lax.axis_size("freq")
    rows = tiles * rank_pad
    u = u_tiles.reshape(rows, width)
    v = v_tiles.reshape(rows, width)
    field = recorded[0]

    def swap(blocks):
        return lax.all_to_all(blocks, "tile", split_axis=0, concat_axis=0, tiled=True)

    out, mine, high_u, low_u = prologue(u, field, tiles, rank_pad)
    out, v = lax.optimization_barrier((out, v))
    wide, short, half = ((rows, traces), F32), ((8, traces), F32), ((rows, rows), BF16)
    kept = (half, half, wide, wide, wide, wide, short)
    out, high_v, low_v, mask_u, mask_v, b0_col, a0, scales = step(
        first_kernel, tiles, rank_pad, kept, "first", tile_ranks[0], v, swap(out)
    )
    out, a1_row, b0, m0 = step(
        second_kernel, tiles, rank_pad, (wide, wide, short), "second", high_u, low_u, mask_u, mine, swap(out)
    )
    out, a1, m1 = step(
        third_kernel, tiles, rank_pad, (wide, short), "third", high_v, low_v, mask_v, a0, b0_col, swap(out)
    )
    known = (high_u, low_u, mask_u, b0, a1_row, scales, m0, m1)
    out, b1, sums = step(fourth_kernel, tiles, rank_pad, (wide, short), "fourth", *known, swap(out))
    blocks = swap(out)
    sums = sums + jnp.sum(blocks[:, rank_pad:].astype(F32), axis=0)
    sums, u, v = lax.optimization_barrier((sums, u, v))
    whole = [sums]
    for shift in range(1, 4):
        whole.append(lax.ppermute(sums, "freq", [(k, k ^ shift) for k in range(freqs)]))
    model, residual, gradient = finish(whole, a0, a1, blocks, b0, b1, v.T, u.T, field, rank_pad)
    return model[None], residual[None], gradient[None]


def by_arrays(u_tiles, v_tiles, tile_ranks, recorded):
    _, tile_dev, tiles, rank_pad, width = u_tiles.shape
    traces = recorded.shape[2]
    freqs = lax.axis_size("freq")
    position = lax.axis_index("tile")
    levels = jnp.arange(rank_pad, dtype=jnp.int32)
    rank_rows = lax.dynamic_slice_in_dim(tile_ranks[0], position * tile_dev, tile_dev, 0)
    rank_cols = lax.dynamic_slice_in_dim(tile_ranks[0], position * tile_dev, tile_dev, 1)
    mask_rows = (levels < rank_rows[..., None]).astype(F32)
    mask_cols = (levels < rank_cols.T[..., None]).astype(F32)
    u = u_tiles[0].reshape(tile_dev, tiles * rank_pad, width)
    v = jnp.swapaxes(v_tiles[0], 0, 1).reshape(tile_dev, tiles * rank_pad, width)
    mask_u = mask_rows.reshape(tile_dev, tiles * rank_pad, 1)
    mask_v = mask_cols.reshape(tile_dev, tiles * rank_pad, 1)

    def gram_of(x):
        return jnp.einsum("drb,dsb->drs", x, x, preferred_element_type=F32)

    def swap(c):
        c = c.reshape(tile_dev, tiles, rank_pad, traces)
        c = lax.all_to_all(c, "tile", split_axis=1, concat_axis=0, tiled=True)
        return jnp.swapaxes(c, 0, 1).reshape(tile_dev, tiles * rank_pad, traces)

    def times(g, c, mask):
        return mask * jnp.einsum("drs,dst->drt", g, c, precision=HIGH)

    field = recorded.reshape(tile_dev, width, traces)
    gram_u, gram_v = gram_of(u), gram_of(v)
    a0 = mask_u * jnp.einsum("drb,dbt->drt", u, field.astype(BF16), preferred_element_type=F32)
    largest = lax.pmax(lax.pmax(jnp.max(jnp.abs(a0)), "tile"), "freq")
    scale = jnp.where(largest > 0.0, largest, 1.0)
    a0 = swap(a0 * (2.0**-20 / scale))
    b0v = times(gram_v, a0, mask_v)
    b0 = swap(b0v)
    a1u = times(gram_u, b0, mask_u)
    a1 = swap(a1u)
    b1v = times(gram_v, a1, mask_v)
    b1 = swap(b1v)
    a2u = times(gram_u, b1, mask_u)
    a2 = swap(a2u)
    parts = jnp.stack([jnp.sum(x * y) for x, y in ((a0, b0v), (b0, a1u), (a1, b1v), (b1, a2u))])
    m0, m1, m2, m3 = lax.psum(lax.psum(parts, "tile"), "freq")
    alpha = m0 / m1
    gamma = m0 - 2.0 * alpha * m1 + alpha * alpha * m2
    grow = 1.0 + gamma / m0
    delta = grow * grow * m1 - 2.0 * alpha * grow * m2 + alpha * alpha * m3
    alpha_new = gamma / delta
    first = alpha + alpha_new * grow
    second = alpha * alpha_new

    def expand(x, c):
        image = jnp.einsum("drb,drt->dbt", x.astype(F32), c, precision=HIGH)
        return image.reshape(1, tile_dev * width, traces)

    back = scale * 2.0**20
    model = back * expand(v, first * a0 - second * a1)
    gradient = back * expand(v, a0 - first * a1 + second * a2)
    residual = recorded - back * expand(u, first * b0 - second * b1)
    return model, residual, gradient


def local(u_tiles, v_tiles, tile_ranks, recorded):
    _, tile_dev, tiles, rank_pad, _ = u_tiles.shape
    small = tile_dev == 1 and tiles * rank_pad <= KERNEL_ROWS and lax.axis_size("freq") == 4
    return (by_kernels if small else by_arrays)(u_tiles, v_tiles, tile_ranks, recorded)


def solution(mesh):
    placed = (
        P("freq", "tile", None, None, None),
        P("freq", None, "tile", None, None),
        P("freq", None, None),
        P("freq", "tile", None),
    )
    out = P("freq", "tile", None)
    return jax.shard_map(local, mesh=mesh, in_specs=placed, out_specs=(out, out, out), check_vma=False)
```
